128 devices in a mesh: tm: 2 (over core), station: 16 (over y, x), channel: 4 (over z).
Axes of the slice: x: 4, y: 4, z: 4, core: 2. Of those that a mesh axis runs over, the one named last changes fastest.
Arguments:
- voltages: bfloat16 [2, 32, 2, 512, 512], P(None, 'channel', None, 'station', 'tm'), may hold values from -64 to 64
- start_seed: int32 [2, 32, 4, 2, 512], P(None, 'channel', None, None, 'station'), may hold values from -8 to 8
- beam_phase: int32 [512, 512], replicated, may hold values from 0 to 1023
- station_delay: int32 [512], replicated, may hold values from 0 to 1023
Outputs:
- beam_output: bfloat16 [2, 32, 2, 512, 512], P(None, 'channel', None, 'station', 'tm')
- subspace: float32 [2, 32, 4, 2, 512], P(None, 'channel', None, None, 'station')
The draws below stay inside these ranges and needn't reach their ends.
All inputs are finite; a program needn't handle non-finite values.
Results may differ from the reference program's by a relative error of at most 0.017.
Values may be sent and summed in bfloat16 or wider, within the bound.
A program may use at most 64 MiB of HBM per device.

```python
import jax
import jax.numpy as jnp
from jax import lax

STATIONS = 512
POLS = 2
CHANNELS = 32
BEAMS = 512
RANK = 4
ITERS = 3
PHASES = 1024
TIME = 512


def draw_voltages(key, part):
    subkeys = jax.random.split(jax.random.fold_in(key, 11), 5)
    full_shape = (2, CHANNELS, POLS, STATIONS, TIME)
    thermal = jax.random.normal(subkeys[0], full_shape, jnp.float32)
    strength = jnp.exp(jax.random.uniform(subkeys[1], (CHANNELS, RANK), jnp.float32, jnp.log(4.0), jnp.log(80.0)))
    amplitude = jnp.exp(jax.random.uniform(subkeys[2], (CHANNELS,), jnp.float32, 0.0, jnp.log(3.3)))
    steering = jax.random.normal(subkeys[3], (2, CHANNELS, RANK, POLS, STATIONS), jnp.float32) * jnp.sqrt(0.5)
    signal = jax.random.normal(subkeys[4], (2, CHANNELS, RANK, TIME), jnp.float32) * jnp.sqrt(0.5)
    strength_root = jnp.sqrt(strength / (POLS * STATIONS))
    signal = signal * strength_root[None, :, :, None]
    pattern = 'ckpm,ckt->cpmt'
    real_sum = jnp.einsum(pattern, steering[0], signal[0]) - jnp.einsum(pattern, steering[1], signal[1])
    imag_sum = jnp.einsum(pattern, steering[0], signal[1]) + jnp.einsum(pattern, steering[1], signal[0])
    growth = jnp.exp(jnp.log(3.0) * jnp.arange(TIME, dtype=jnp.float32) / TIME)
    envelope = amplitude[:, None, None, None] * growth[None, None, None, :]
    voltage = (thermal + jnp.stack([real_sum, imag_sum])) * envelope[None]
    return jnp.clip(voltage, -64.0, 64.0).astype(jnp.bfloat16)


def set_ends(array, stream_key, low, high):
    extent = array.shape
    index_at = [jax.random.randint(jax.random.fold_in(stream_key, axis), (), 0, extent[axis]) for axis in range(len(extent))]
    array = array.at[tuple(index_at)].set(low)
    longest = extent.index(max(extent))
    index_at[longest] = (index_at[longest] + 1) % extent[longest]
    return array.at[tuple(index_at)].set(high)


def setup_inputs(seed: int = 0) -> dict:
    key_of = jax.random.split(jax.random.key(seed), 5)
    return {
        "voltages": draw_voltages(jax.random.fold_in(key_of[4], 71), 0),
        "start_seed": set_ends(jax.random.randint(key_of[1], (2, CHANNELS, RANK, POLS, STATIONS), -8, 9), jax.random.fold_in(key_of[1], 1), -8, 8).astype(jnp.int32),
        "beam_phase": set_ends(jax.random.randint(key_of[2], (BEAMS, STATIONS), 0, PHASES), jax.random.fold_in(key_of[2], 1), 0, PHASES - 1).astype(jnp.int32),
        "station_delay": set_ends(jax.random.randint(key_of[3], (STATIONS,), 0, PHASES), jax.random.fold_in(key_of[3], 1), 0, PHASES - 1).astype(jnp.int32),
    }


HIGH = lax.Precision.HIGHEST

def coefficients(subspace, voltage):
    real_v = voltage[0].astype(jnp.float32)
    imag_v = voltage[1].astype(jnp.float32)
    pattern = '...kpm,...pmt->...kt'
    real_sum = jnp.einsum(pattern, subspace[0], real_v, precision=HIGH) + jnp.einsum(pattern, subspace[1], imag_v, precision=HIGH)
    imag_sum = jnp.einsum(pattern, subspace[0], imag_v, precision=HIGH) - jnp.einsum(pattern, subspace[1], real_v, precision=HIGH)
    return jnp.stack([real_sum, imag_sum])

def applied(voltage, coefficient):
    real_v = voltage[0].astype(jnp.float32)
    imag_v = voltage[1].astype(jnp.float32)
    pattern = '...pmt,...kt->...kpm'
    real_sum = jnp.einsum(pattern, real_v, coefficient[0], precision=HIGH) + jnp.einsum(pattern, imag_v, coefficient[1], precision=HIGH)
    imag_sum = jnp.einsum(pattern, imag_v, coefficient[0], precision=HIGH) - jnp.einsum(pattern, real_v, coefficient[1], precision=HIGH)
    return jnp.stack([real_sum, imag_sum])

def gram_matrix(image_field):
    pattern = '...kpm,...lpm->...kl'
    real_sum = jnp.einsum(pattern, image_field[0], image_field[0], precision=HIGH) + jnp.einsum(pattern, image_field[1], image_field[1], precision=HIGH)
    imag_sum = jnp.einsum(pattern, image_field[0], image_field[1], precision=HIGH) - jnp.einsum(pattern, image_field[1], image_field[0], precision=HIGH)
    return jnp.stack([real_sum, imag_sum])

def inverse_factor(gram_real, gram_imag):
    rank_count = gram_real.shape[-1]
    nothing = jnp.zeros_like(gram_real[..., 0, 0])
    low_real = {}
    low_imag = {}
    for column in range(rank_count):
        diagonal = gram_real[..., column, column]
        for middle in range(column):
            diagonal = diagonal - low_real[column, middle] ** 2 - low_imag[column, middle] ** 2
        pivot_root = jnp.sqrt(diagonal)
        low_real[column, column] = pivot_root
        low_imag[column, column] = nothing
        for row_at in range(column + 1, rank_count):
            acc_real = gram_real[..., row_at, column]
            acc_imag = gram_imag[..., row_at, column]
            for middle in range(column):
                acc_real = acc_real - (low_real[row_at, middle] * low_real[column, middle] + low_imag[row_at, middle] * low_imag[column, middle])
                acc_imag = acc_imag - (low_imag[row_at, middle] * low_real[column, middle] - low_real[row_at, middle] * low_imag[column, middle])
            low_real[row_at, column] = acc_real / pivot_root
            low_imag[row_at, column] = acc_imag / pivot_root
    inv_real = {}
    inv_imag = {}
    for column in range(rank_count):
        inv_real[column, column] = 1.0 / low_real[column, column]
        inv_imag[column, column] = nothing
        for row_at in range(column + 1, rank_count):
            acc_real = nothing
            acc_imag = nothing
            for middle in range(column, row_at):
                acc_real = acc_real + low_real[row_at, middle] * inv_real[middle, column] - low_imag[row_at, middle] * inv_imag[middle, column]
                acc_imag = acc_imag + low_real[row_at, middle] * inv_imag[middle, column] + low_imag[row_at, middle] * inv_real[middle, column]
            inv_real[row_at, column] = -acc_real / low_real[row_at, row_at]
            inv_imag[row_at, column] = -acc_imag / low_real[row_at, row_at]
    real_rows = [jnp.stack([inv_real.get((row_at, column), nothing) for column in range(rank_count)], axis=-1) for row_at in range(rank_count)]
    imag_rows = [jnp.stack([inv_imag.get((row_at, column), nothing) for column in range(rank_count)], axis=-1) for row_at in range(rank_count)]
    return (jnp.stack(real_rows, axis=-2), jnp.stack(imag_rows, axis=-2))

def orthonormal(image_field, sums):
    inv_real, inv_imag = inverse_factor(sums[0], sums[1])
    pattern = '...lpm,...kl->...kpm'
    real_sum = jnp.einsum(pattern, image_field[0], inv_real, precision=HIGH) + jnp.einsum(pattern, image_field[1], inv_imag, precision=HIGH)
    imag_sum = jnp.einsum(pattern, image_field[1], inv_real, precision=HIGH) - jnp.einsum(pattern, image_field[0], inv_imag, precision=HIGH)
    return jnp.stack([real_sum, imag_sum])

def project_out(voltage, subspace, coefficient):
    pattern = '...kpm,...kt->...pmt'
    real_sum = jnp.einsum(pattern, subspace[0], coefficient[0], precision=HIGH) - jnp.einsum(pattern, subspace[1], coefficient[1], precision=HIGH)
    imag_sum = jnp.einsum(pattern, subspace[0], coefficient[1], precision=HIGH) + jnp.einsum(pattern, subspace[1], coefficient[0], precision=HIGH)
    return jnp.stack([voltage[0].astype(jnp.float32) - real_sum, voltage[1].astype(jnp.float32) - imag_sum])

def beam_weights(phase_rows, delays, channel_numbers):
    summed = phase_rows + delays[None, :]
    index = summed[None, :, :] * (channel_numbers[:, None, None] + 1) % PHASES
    angle = index.astype(jnp.float32) * (2.0 * jnp.pi / PHASES)
    norming = 1.0 / jnp.sqrt(jnp.float32(STATIONS))
    return ((jnp.cos(angle) * norming).astype(jnp.bfloat16), (-jnp.sin(angle) * norming).astype(jnp.bfloat16))

def form_beams(real_w, imag_w, cleaned):
    pattern = '...bm,...pmt->...pbt'
    real_w = real_w.astype(jnp.float32)
    imag_w = imag_w.astype(jnp.float32)
    real_c = cleaned[0].astype(jnp.float32)
    imag_c = cleaned[1].astype(jnp.float32)
    real_sum = jnp.einsum(pattern, real_w, real_c, precision=HIGH) - jnp.einsum(pattern, imag_w, imag_c, precision=HIGH)
    imag_sum = jnp.einsum(pattern, real_w, imag_c, precision=HIGH) + jnp.einsum(pattern, imag_w, real_c, precision=HIGH)
    return jnp.stack([real_sum, imag_sum])

def reference(voltages, start_seed, beam_phase, station_delay):

    def per_channel(inputs):
        voltage, start_field, channel_number = inputs
        subspace = start_field.astype(jnp.float32)
        for iteration in range(ITERS):
            summed = applied(voltage, coefficients(subspace, voltage))
            subspace = orthonormal(summed, gram_matrix(summed))
        cleaned = project_out(voltage, subspace, coefficients(subspace, voltage)).astype(jnp.bfloat16)
        real_w, imag_w = beam_weights(beam_phase, station_delay, channel_number.reshape(1))
        beam_field = form_beams(real_w[0], imag_w[0], cleaned)
        return (subspace, beam_field)
    numbers = jnp.arange(CHANNELS, dtype=jnp.int32)
    subspace_all, beams_all = lax.map(per_channel, (jnp.moveaxis(voltages, 1, 0), jnp.moveaxis(start_seed, 1, 0), numbers))
    beam_power = lax.optimization_barrier(jnp.sum(beams_all[:, 0] ** 2 + beams_all[:, 1] ** 2, axis=(0, 3))) / (CHANNELS * TIME)
    rescale = lax.rsqrt(beam_power + 1e-06)
    beam_output = (beams_all * rescale[None, None, :, :, None]).astype(jnp.bfloat16)
    return (jnp.moveaxis(beam_output, 0, 1), jnp.moveaxis(subspace_all, 0, 1))
```

```python
import functools

import jax
import jax.numpy as jnp
from jax import lax
from jax.experimental import pallas as pl
from jax.experimental.pallas import tpu as pltpu
from jax.sharding import PartitionSpec as P

STATIONS = 512
CHANNELS = 32
ITERS = 3
PHASES = 1024
TIME = 512
RANK = 4
GROUP = 16
QUARTERS = 4

MESH = pl.DeviceIdType.MESH

COS_TERMS = (
    0.9999999998855527,
    -4.934802185863431,
    4.058711817242859,
    -1.3352602861671086,
    0.23532082553812417,
    -0.025785808775470303,
    0.0019043289643584185,
    -8.86909374720357e-05,
)
SIN_TERMS = (
    3.141592653568331,
    -5.167712777297557,
    2.5501639819324518,
    -0.599264064211247,
    0.0821440508162118,
    -0.007366486943808629,
    0.000461586777512204,
    -1.8944663042615234e-05,
)


def horner(terms, scale, v):
    total = jnp.full_like(v, terms[-1] * scale)
    for term in terms[-2::-1]:
        total = total * v + jnp.float32(term * scale)
    return total


def three_parts(value):
    high = value.astype(jnp.bfloat16)
    rest = value - high.astype(jnp.float32)
    middle = rest.astype(jnp.bfloat16)
    low = (rest - middle.astype(jnp.float32)).astype(jnp.bfloat16)
    return high, middle, low


def sum_of_three(rows):
    return rows[0:8] + (rows[8:16] + rows[16:24])


def half_swap(rows):
    return pltpu.roll(rows, 4, 0)


def kernel(
    volt,
    seed,
    phase,
    delay,
    out,
    sub,
    local_x,
    phases,
    field,
    first_out,
    first_in,
    image,
    weights,
    product,
    stage,
    power_out,
    power_in,
    power_two,
    basis_out,
    basis_in,
    arrived,
    result,
    local_sem,
    send_x,
    recv_x,
    send_first,
    recv_first,
    send_image,
    recv_image,
    send_basis,
    recv_basis,
    send_power,
    recv_power,
    send_two,
    recv_two,
    send_beam,
    recv_beam,
    out_sem,
):
    core = lax.axis_index("tm")
    me = lax.axis_index("station")
    plane = lax.axis_index("channel")
    mine = me // 2
    half = me % 2
    twin = me + 1 - 2 * half
    quarter = core * 2 + half

    def partner(step):
        row = (me // 4 + step // 4) % 4
        column = (me % 4 + step % 4) % 4
        return row * 4 + column

    def rows_of(station, size):
        return pl.ds(pl.multiple_of(station * size, size), size)

    def lanes_of(which):
        return pl.ds(pl.multiple_of(which * 128, 128), 128)

    load_x = pltpu.make_async_copy(volt, local_x, local_sem.at[0])
    load_x.start()
    load_phase = pltpu.make_async_copy(phase, phases, local_sem.at[1])
    load_phase.start()

    barrier = pltpu.get_barrier_semaphore()
    three = (
        {"tm": 1 - core},
        {"station": twin},
        {"tm": 1 - core, "station": twin},
    )
    seven = [{"tm": 1 - core}]
    for step in range(1, 4):
        other = (plane + step) % 4
        seven.append({"channel": other})
        seven.append({"tm": 1 - core, "channel": other})

    def greet(step, carry):
        pl.semaphore_signal(barrier, inc=1, device_id={"station": partner(step)}, device_id_type=MESH)
        return carry

    lax.fori_loop(1, GROUP, greet, 0)
    for peer in seven:
        pl.semaphore_signal(barrier, inc=1, device_id=peer, device_id_type=MESH)
    pl.semaphore_signal(barrier, inc=1, device_id=three[2], device_id_type=MESH)
    pl.semaphore_wait(barrier, GROUP - 1 + len(seven) + 1)

    def x_copy(step, part):
        peer = partner(step)
        return pltpu.make_async_remote_copy(
            src_ref=volt.at[part, peer // 2, :, :, lanes_of(peer % 2)],
            dst_ref=field.at[:, rows_of(me, 32), pl.ds(part * 128, 128)],
            send_sem=send_x.at[part, step],
            recv_sem=recv_x.at[part, me],
            device_id={"station": peer},
            device_id_type=MESH,
        )

    def x_start(step, carry):
        x_copy(step, 0).start()
        x_copy(step, 1).start()
        return carry

    lax.fori_loop(1, GROUP, x_start, 0)
    own_x = [
        pltpu.make_async_copy(
            volt.at[part, mine, :, :, lanes_of(half)],
            field.at[:, rows_of(me, 32), pl.ds(part * 128, 128)],
            local_sem.at[2 + part],
        )
        for part in range(2)
    ]
    for copy in own_x:
        copy.start()

    load_x.wait()
    for c in range(8):
        total = jnp.zeros((8, 256), jnp.float32)
        for p in range(2):
            real_s = seed[0, c, pl.ds(p, 4, stride=2), :].astype(jnp.float32)
            imag_s = seed[1, c, pl.ds(p, 4, stride=2), :].astype(jnp.float32)
            on_real = jnp.concatenate([real_s, -imag_s], axis=0).astype(jnp.bfloat16)
            on_imag = jnp.concatenate([imag_s, real_s], axis=0).astype(jnp.bfloat16)
            total += jnp.dot(on_real, local_x[0, c, p], preferred_element_type=jnp.float32)
            total += jnp.dot(on_imag, local_x[1, c, p], preferred_element_type=jnp.float32)
        first_out[2 * c] = total[:, 0:128]
        first_out[2 * c + 1] = total[:, 128:256]

    def first_copy(step):
        peer = partner(step)
        return pltpu.make_async_remote_copy(
            src_ref=first_out.at[peer],
            dst_ref=first_in.at[me],
            send_sem=send_first.at[step],
            recv_sem=recv_first.at[me],
            device_id={"station": peer},
            device_id_type=MESH,
        )

    def first_start(step, carry):
        first_copy(step).start()
        return carry

    lax.fori_loop(1, GROUP, first_start, 0)
    first_in[me] = first_out[me]

    load_phase.wait()
    number = plane * 8 + mine + 1
    norming = STATIONS**-0.5

    def weight_rows(block, carry):
        rows = rows_of(block, 32)
        index = (phases[rows, :] + delay[...]) * number
        wrapped = (index + PHASES // 2) & (PHASES - 1)
        u = (wrapped - PHASES // 2).astype(jnp.float32) * jnp.float32(2.0 / PHASES)
        v = u * u
        weights[0, rows, :] = horner(COS_TERMS, norming, v).astype(jnp.bfloat16)
        weights[1, rows, :] = (u * horner(SIN_TERMS, -norming, v)).astype(jnp.bfloat16)
        return carry

    lax.fori_loop(0, 16, weight_rows, 0)

    def arrive(step, carry):
        source = partner(step)
        for part in range(2):
            pltpu.make_async_remote_copy(
                src_ref=volt.at[part, mine, :, :, lanes_of(half)],
                dst_ref=field.at[:, rows_of(source, 32), pl.ds(part * 128, 128)],
                send_sem=send_x.at[part, step],
                recv_sem=recv_x.at[part, source],
                device_id={"station": source},
                device_id_type=MESH,
            ).wait_recv()
        pltpu.make_async_remote_copy(
            src_ref=first_out.at[source],
            dst_ref=first_in.at[source],
            send_sem=send_first.at[step],
            recv_sem=recv_first.at[source],
            device_id={"station": source},
            device_id_type=MESH,
        ).wait_recv()
        return carry

    lax.fori_loop(1, GROUP, arrive, 0)
    for copy in own_x:
        copy.wait()

    row = lax.broadcasted_iota(jnp.int32, (8, 128), 0)
    upper = jnp.where(row < 4, 1.0, -1.0).astype(jnp.float32)

    def turned(c8):
        return jnp.concatenate([c8, half_swap(c8) * upper], axis=1)

    def apply_field(c8):
        left = jnp.concatenate(three_parts(turned(c8)), axis=0)
        right = field[...].reshape(1024, 256)
        rows = lax.dot_general(left, right, (((1,), (1,)), ((), ())), preferred_element_type=jnp.float32)
        return sum_of_three(rows)

    def coefficients(h8):
        left = jnp.concatenate(three_parts(h8), axis=0)
        rows = jnp.dot(left, field[...].reshape(1024, 256), preferred_element_type=jnp.float32)
        rows = sum_of_three(rows)
        return rows[:, 0:128] - upper * half_swap(rows[:, 128:256])

    def factor(h8):
        shifted = []
        for shift in range(4):
            moved = h8 * (pltpu.roll(h8, shift, 0) if shift else h8)
            lanes = moved[:, 0:128]
            for block in range(1, 8):
                lanes = lanes + moved[:, block * 128 : (block + 1) * 128]
            dots = jnp.broadcast_to(jnp.sum(lanes, axis=1, keepdims=True), (8, 128))
            swapped = half_swap(dots)
            shifted.append((dots + swapped, dots - swapped))

        def pick(rows, at):
            return jnp.broadcast_to(rows[at : at + 1, :], (8, 128))

        low = {}
        inverse = {}
        for column in range(RANK):
            diagonal = pick(shifted[0][0], column)
            for middle in range(column):
                re, im = low[column, middle]
                diagonal = diagonal - (re * re + im * im)
            inverse[column] = lax.rsqrt(diagonal)
            for at in range(column + 1, RANK):
                distance = at - column
                re = pick(shifted[distance][0], at)
                im = pick(shifted[4 - distance][1], column)
                for middle in range(column):
                    a_re, a_im = low[at, middle]
                    b_re, b_im = low[column, middle]
                    re = re - (a_re * b_re + a_im * b_im)
                    im = im - (a_im * b_re - a_re * b_im)
                low[at, column] = (re * inverse[column], im * inverse[column])
        return low, inverse

    def solve(low, inverse, rows):
        width = rows.shape[1]
        repeat = width // 128

        def wide(value):
            return value if repeat == 1 else jnp.concatenate([value] * repeat, axis=1)

        done = []
        for at in range(RANK):
            re = jnp.broadcast_to(rows[at : at + 1, :], (8, width))
            im = jnp.broadcast_to(rows[at + 4 : at + 5, :], (8, width))
            for middle in range(at):
                l_re, l_im = low[at, middle]
                l_re, l_im = wide(l_re), wide(l_im)
                d_re, d_im = done[middle]
                re = re - (l_re * d_re - l_im * d_im)
                im = im - (l_re * d_im + l_im * d_re)
            scale = wide(inverse[at])
            done.append((re * scale, im * scale))
        at_row = lax.broadcasted_iota(jnp.int32, (8, width), 0)
        total = done[3][1]
        for at in range(RANK):
            total = jnp.where(at_row == at, done[at][0], total)
            if at < 3:
                total = jnp.where(at_row == at + 4, done[at][1], total)
        return total

    coefficient = first_in[0]
    for station in range(1, GROUP):
        coefficient = coefficient + first_in[station]

    image_copies = []
    for iteration in range(ITERS):
        image[iteration, quarter] = apply_field(coefficient)
        for at, peer in enumerate(three):
            copy = pltpu.make_async_remote_copy(
                src_ref=image.at[iteration, quarter],
                dst_ref=image.at[iteration, quarter],
                send_sem=send_image.at[iteration, at],
                recv_sem=recv_image.at[iteration, at],
                device_id=peer,
                device_id_type=MESH,
            )
            copy.start()
            image_copies.append(copy)
        for copy in image_copies[-3:]:
            copy.wait_recv()
        summed = (image[iteration, 0] + image[iteration, 1]) + (image[iteration, 2] + image[iteration, 3])
        raw = coefficients(summed)
        low, inverse = factor(summed)
        coefficient = solve(low, inverse, raw)
    basis = solve(low, inverse, summed)

    for p in range(2):
        for block in range(4):
            lanes = basis[:, p * 512 + block * 128 : p * 512 + (block + 1) * 128] * upper
            for inner in range(4):
                moved = pltpu.roll(lanes, 128 - 32 * inner, 1) if inner else lanes
                basis_out[block * 4 + inner, p * 8 : (p + 1) * 8, :] = moved

    def basis_copy(step, slot, peer):
        return pltpu.make_async_remote_copy(
            src_ref=basis_out.at[peer],
            dst_ref=basis_in.at[slot],
            send_sem=send_basis.at[step],
            recv_sem=recv_basis.at[slot],
            device_id={"station": peer},
            device_id_type=MESH,
        )

    def basis_start(step, carry):
        peer = partner(step)

        @pl.when(peer // 8 == half)
        def _():
            basis_copy(step, mine, peer).start()

        return carry

    def six(parts, which):
        return jnp.concatenate([parts[at] for at in which], axis=0)

    basis_parts = three_parts(basis)
    coefficient_parts = three_parts(turned(coefficient))
    left = six(basis_parts, (0, 0, 1, 0, 1, 2))
    right = six(coefficient_parts, (0, 1, 0, 2, 1, 0))
    removed = lax.dot_general(left, right, (((0,), (0,)), ((), ())), preferred_element_type=jnp.float32)
    cleaned = field[...].reshape(1024, 256).astype(jnp.float32) - removed
    cleaned = cleaned.astype(jnp.bfloat16)
    for p in range(2):
        ours = cleaned[p * 512 : (p + 1) * 512]
        on_real = jnp.dot(weights[0], ours, preferred_element_type=jnp.float32)
        on_imag = jnp.dot(weights[1], ours, preferred_element_type=jnp.float32)
        product[p, :, 0:128] = on_real[:, 0:128] - on_imag[:, 128:256]
        product[p, :, 128:256] = on_real[:, 128:256] + on_imag[:, 0:128]

    def beam_copy(step, peer):
        return pltpu.make_async_remote_copy(
            src_ref=stage.at[:, :, rows_of(peer, 32), :],
            dst_ref=arrived.at[:, mine, :, :, lanes_of(half)],
            send_sem=send_beam.at[step],
            recv_sem=recv_beam.at[me],
            device_id={"station": peer},
            device_id_type=MESH,
        )

    def power_copy(step, peer):
        return pltpu.make_async_remote_copy(
            src_ref=power_out.at[peer],
            dst_ref=power_in.at[me],
            send_sem=send_power.at[step],
            recv_sem=recv_power.at[me],
            device_id={"station": peer},
            device_id_type=MESH,
        )

    lane_group = lax.broadcasted_iota(jnp.int32, (8, 128), 1) // 16

    def finish_block(peer):
        rows = rows_of(peer, 32)
        compact = jnp.zeros((8, 128), jnp.float32)
        for p in range(2):
            real_b = product[p, rows, 0:128]
            imag_b = product[p, rows, 128:256]
            stage[0, p, rows, :] = real_b.astype(jnp.bfloat16)
            stage[1, p, rows, :] = imag_b.astype(jnp.bfloat16)
            squares = jnp.sum(real_b * real_b + imag_b * imag_b, axis=1, keepdims=True)
            for block in range(4):
                compact = jnp.where(
                    lane_group == p * 4 + block,
                    jnp.broadcast_to(squares[block * 8 : (block + 1) * 8], (8, 128)),
                    compact,
                )
        power_out[peer] = compact

    def beam_start(step, carry):
        peer = partner(step)
        finish_block(peer)
        power_copy(step, peer).start()
        beam_copy(step, peer).start()
        return carry

    lax.fori_loop(1, GROUP, beam_start, 0)
    finish_block(me)
    power_in[me] = power_out[me]
    own_beam = pltpu.make_async_copy(
        stage.at[:, :, rows_of(me, 32), :],
        arrived.at[:, mine, :, :, lanes_of(half)],
        local_sem.at[4],
    )
    own_beam.start()

    lax.fori_loop(1, GROUP, basis_start, 0)

    @pl.when(me // 8 == half)
    def _():
        basis_in[mine] = basis_out[me]

    def power_arrive(step, carry):
        source = partner(step)
        pltpu.make_async_remote_copy(
            src_ref=power_out.at[source],
            dst_ref=power_in.at[source],
            send_sem=send_power.at[step],
            recv_sem=recv_power.at[source],
            device_id={"station": source},
            device_id_type=MESH,
        ).wait_recv()
        return carry

    lax.fori_loop(1, GROUP, power_arrive, 0)
    power = power_in[0]
    for station in range(1, GROUP):
        power = power + power_in[station]
    slot = plane * 2 + core
    power_two[slot] = power
    two_copies = []
    for at, peer in enumerate(seven):
        copy = pltpu.make_async_remote_copy(
            src_ref=power_two.at[slot],
            dst_ref=power_two.at[slot],
            send_sem=send_two.at[at],
            recv_sem=recv_two.at[at],
            device_id=peer,
            device_id_type=MESH,
        )
        copy.start()
        two_copies.append(copy)
    for copy in two_copies:
        copy.wait_recv()
    power = power_two[0]
    for at in range(1, 8):
        power = power + power_two[at]
    rescale = lax.rsqrt(power / (CHANNELS * TIME) + 1e-06)

    for c in range(8):

        @pl.when(2 * c + me // 8 != me)
        def _():
            basis_copy(0, c, 2 * c + me // 8).wait_recv()

    for c in range(8):
        for p in range(2):
            for part in range(2):
                at = p * 8 + part * 4
                sub[part, c, pl.ds(p, 4, stride=2), :] = basis_in[c, at : at + 4, 0:32]

    def beam_arrive(step, carry):
        source = partner(step)
        pltpu.make_async_remote_copy(
            src_ref=stage.at[:, :, rows_of(me, 32), :],
            dst_ref=arrived.at[:, source // 2, :, :, lanes_of(source % 2)],
            send_sem=send_beam.at[step],
            recv_sem=recv_beam.at[source],
            device_id={"station": source},
            device_id_type=MESH,
        ).wait_recv()
        return carry

    lax.fori_loop(1, GROUP, beam_arrive, 0)
    own_beam.wait()

    scales = []
    for p in range(2):
        rows = []
        for block in range(4):
            lane = (p * 4 + block) * 16
            rows.append(jnp.broadcast_to(rescale[:, lane : lane + 1], (8, 256)))
        scales.append(jnp.concatenate(rows, axis=0))

    def out_copy(c):
        return pltpu.make_async_copy(result.at[:, c], out.at[:, c], out_sem.at[c])

    def normalise(c, carry):
        for part in range(2):
            for p in range(2):
                value = arrived[part, c, p].astype(jnp.float32) * scales[p]
                result[part, c, p] = value.astype(jnp.bfloat16)
        out_copy(c).start()
        return carry

    lax.fori_loop(0, 8, normalise, 0)

    def drain(step, carry):
        peer = partner(step)
        x_copy(step, 0).wait_send()
        x_copy(step, 1).wait_send()
        first_copy(step).wait_send()
        power_copy(step, peer).wait_send()
        beam_copy(step, peer).wait_send()

        @pl.when(peer // 8 == half)
        def _():
            basis_copy(step, mine, peer).wait_send()

        return carry

    lax.fori_loop(1, GROUP, drain, 0)
    for copy in image_copies + two_copies:
        copy.wait_send()

    def out_wait(c, carry):
        out_copy(c).wait()
        return carry

    lax.fori_loop(0, 8, out_wait, 0)


def body(voltages, start_seed, beam_phase, station_delay):
    vmem = pl.BlockSpec(memory_space=pltpu.VMEM)
    anywhere = pl.BlockSpec(memory_space=pl.ANY)
    dma = pltpu.SemaphoreType.DMA
    f32, bf16 = jnp.float32, jnp.bfloat16
    beam_output, subspace = pl.pallas_call(
        kernel,
        out_shape=(
            jax.ShapeDtypeStruct((2, 8, 2, 32, 256), bf16),
            jax.ShapeDtypeStruct((2, 8, 8, 32), f32),
        ),
        in_specs=[anywhere, vmem, anywhere, vmem],
        out_specs=(anywhere, vmem),
        scratch_shapes=[
            pltpu.VMEM((2, 8, 2, 32, 256), bf16),
            pltpu.VMEM((512, 512), jnp.int32),
            pltpu.VMEM((2, 512, 256), bf16),
            pltpu.VMEM((16, 8, 128), f32),
            pltpu.VMEM((16, 8, 128), f32),
            pltpu.VMEM((ITERS, QUARTERS, 8, 1024), f32),
            pltpu.VMEM((2, 512, 512), bf16),
            pltpu.VMEM((2, 512, 256), f32),
            pltpu.VMEM((2, 2, 512, 128), bf16),
            pltpu.VMEM((16, 8, 128), f32),
            pltpu.VMEM((16, 8, 128), f32),
            pltpu.VMEM((8, 8, 128), f32),
            pltpu.VMEM((16, 16, 128), f32),
            pltpu.VMEM((8, 16, 128), f32),
            pltpu.VMEM((2, 8, 2, 32, 256), bf16),
            pltpu.VMEM((2, 8, 2, 32, 256), bf16),
            dma((5,)),
            dma((2, 16)),
            dma((2, 16)),
            dma((16,)),
            dma((16,)),
            dma((ITERS, 3)),
            dma((ITERS, 3)),
            dma((16,)),
            dma((8,)),
            dma((16,)),
            dma((16,)),
            dma((7,)),
            dma((7,)),
            dma((16,)),
            dma((16,)),
            dma((8,)),
        ],
        compiler_params=pltpu.CompilerParams(
            collective_id=0, has_side_effects=True, vmem_limit_bytes=40 * 1024 * 1024
        ),
    )(
        voltages,
        start_seed.reshape(2, 8, 8, 32),
        beam_phase,
        station_delay.reshape(1, STATIONS),
    )
    return beam_output, subspace.reshape(2, 8, 4, 2, 32)


def solution(mesh):
    in_specs = (
        P(None, "channel", None, "station", "tm"),
        P(None, "channel", None, None, "station"),
        P(),
        P(),
    )
    out_specs = (
        P(None, "channel", None, "station", "tm"),
        P(None, "channel", None, None, "station"),
    )
    return jax.shard_map(body, mesh=mesh, in_specs=in_specs, out_specs=out_specs, check_vma=False)
```

```python
import functools

import jax
import jax.numpy as jnp
from jax import lax
from jax.experimental import pallas as pl
from jax.experimental.pallas import tpu as pltpu
from jax.sharding import PartitionSpec as P

STATIONS = 512
CHANNELS = 32
ITERS = 3
PHASES = 1024
TIME = 512
RANK = 4
GROUP = 16
QUARTERS = 4

MESH = pl.DeviceIdType.MESH

COS_TERMS = (
    0.9999999998855527,
    -4.934802185863431,
    4.058711817242859,
    -1.3352602861671086,
    0.23532082553812417,
    -0.025785808775470303,
    0.0019043289643584185,
    -8.86909374720357e-05,
)
SIN_TERMS = (
    3.141592653568331,
    -5.167712777297557,
    2.5501639819324518,
    -0.599264064211247,
    0.0821440508162118,
    -0.007366486943808629,
    0.000461586777512204,
    -1.8944663042615234e-05,
)


def horner(terms, scale, v):
    total = jnp.full_like(v, terms[-1] * scale)
    for term in terms[-2::-1]:
        total = total * v + jnp.float32(term * scale)
    return total


def three_parts(value):
    high = value.astype(jnp.bfloat16)
    rest = value - high.astype(jnp.float32)
    middle = rest.astype(jnp.bfloat16)
    low = (rest - middle.astype(jnp.float32)).astype(jnp.bfloat16)
    return high, middle, low


def sum_of_three(rows):
    return rows[0:8] + (rows[8:16] + rows[16:24])


def half_swap(rows):
    return pltpu.roll(rows, 4, 0)


def exchange(
    volt,
    seed_hbm,
    phase,
    delay_hbm,
    arrived,
    rescale,
    basis_in,
    local_x,
    seed,
    phases,
    delay,
    field,
    first_out,
    first_in,
    image,
    weights,
    stage,
    power_out,
    power_in,
    power_two,
    basis_out,
    local_sem,
    send_x,
    recv_x,
    send_first,
    recv_first,
    send_image,
    recv_image,
    send_basis,
    recv_basis,
    send_power,
    recv_power,
    send_two,
    recv_two,
    send_beam,
    recv_beam,
):
    core = lax.axis_index("tm")
    me = lax.axis_index("station")
    plane = lax.axis_index("channel")
    mine = me // 2
    half = me % 2
    twin = me + 1 - 2 * half
    quarter = core * 2 + half

    def partner(step):
        across = (step // 4 + 2) % 4
        along = (step % 4 + 2) % 4
        row = (me // 4 + across) % 4
        column = (me % 4 + along) % 4
        return row * 4 + column

    def everyone(start):
        lax.fori_loop(0, 10, lambda step, carry: start(step) or carry, 0)
        lax.fori_loop(11, GROUP, lambda step, carry: start(step) or carry, 0)

    loads = [
        pltpu.make_async_copy(
            volt.at[part, :, :, :, pl.ds(side * 128, 128)],
            local_x.at[:, side, :, :, pl.ds(part * 128, 128)],
            local_sem.at[part * 2 + side],
        )
        for part in range(2)
        for side in range(2)
    ]
    loads.append(pltpu.make_async_copy(seed_hbm, seed, local_sem.at[4]))
    loads.append(pltpu.make_async_copy(phase, phases, local_sem.at[5]))
    loads.append(pltpu.make_async_copy(delay_hbm, delay, local_sem.at[6]))

    barrier = pltpu.get_barrier_semaphore()
    three = (
        {"tm": 1 - core, "station": twin},
        {"station": twin},
        {"tm": 1 - core},
    )
    seven = [{"channel": (plane + 2) % 4}, {"tm": 1 - core, "channel": (plane + 2) % 4}]
    for step in (1, 3):
        other = (plane + step) % 4
        seven.append({"channel": other})
        seven.append({"tm": 1 - core, "channel": other})
    seven.append({"tm": 1 - core})

    def greet(peer):
        pl.semaphore_signal(barrier, inc=1, device_id=peer, device_id_type=MESH)

    everyone(lambda step: greet({"station": partner(step)}))
    for peer in seven:
        greet(peer)
    greet(three[0])
    for load in loads:
        load.start()
    for load in loads[:4]:
        load.wait()
    pl.semaphore_wait(barrier, GROUP - 1 + len(seven) + 1)

    def x_copy(step, peer, slot):
        return pltpu.make_async_remote_copy(
            src_ref=local_x.at[peer // 2, peer % 2],
            dst_ref=field.at[slot],
            send_sem=send_x.at[step],
            recv_sem=recv_x.at[slot],
            device_id={"station": peer},
            device_id_type=MESH,
        )

    everyone(lambda step: x_copy(step, partner(step), me).start())
    own_x = pltpu.make_async_copy(local_x.at[mine, half], field.at[me], local_sem.at[7])
    own_x.start()

    row = lax.broadcasted_iota(jnp.int32, (8, 128), 0)
    upper = jnp.where(row < 4, 1.0, -1.0).astype(jnp.float32)

    loads[4].wait()
    for c in range(8):
        left = []
        for p in range(2):
            real_s = seed[0, c, pl.ds(p, 4, stride=2), :].astype(jnp.float32)
            imag_s = seed[1, c, pl.ds(p, 4, stride=2), :].astype(jnp.float32)
            left.append(jnp.concatenate([real_s, imag_s], axis=0))
        left = jnp.concatenate(left, axis=1).astype(jnp.bfloat16)
        for side in range(2):
            right = local_x[c, side].reshape(64, 256)
            rows = jnp.dot(left, right, preferred_element_type=jnp.float32)
            first_out[2 * c + side] = half_swap(rows[:, 128:256]) + upper * rows[:, 0:128]

    def first_copy(step, peer, slot):
        return pltpu.make_async_remote_copy(
            src_ref=first_out.at[peer],
            dst_ref=first_in.at[slot],
            send_sem=send_first.at[step],
            recv_sem=recv_first.at[slot],
            device_id={"station": peer},
            device_id_type=MESH,
        )

    everyone(lambda step: first_copy(step, partner(step), me).start())
    first_in[me] = first_out[me]

    loads[5].wait()
    loads[6].wait()
    number = plane * 8 + mine + 1
    norming = STATIONS**-0.5

    def weight_rows(block, carry):
        rows = pl.ds(pl.multiple_of(block * 32, 32), 32)
        index = (phases[rows, :] + delay[...]) * number
        wrapped = (index + PHASES // 2) & (PHASES - 1)
        u = (wrapped - PHASES // 2).astype(jnp.float32) * jnp.float32(2.0 / PHASES)
        v = u * u
        weights[0, rows, :] = horner(COS_TERMS, norming, v).astype(jnp.bfloat16)
        weights[1, rows, :] = (u * horner(SIN_TERMS, -norming, v)).astype(jnp.bfloat16)
        return carry

    lax.fori_loop(0, 16, weight_rows, 0)

    def arrive(step):
        source = partner(step)
        first_copy(step, source, source).wait_recv()
        x_copy(step, source, source).wait_recv()

    everyone(arrive)
    own_x.wait()

    def turned(c8):
        return jnp.concatenate([c8, half_swap(c8) * upper], axis=1)

    def apply_field(c8):
        left = jnp.concatenate(three_parts(turned(c8)), axis=0)
        right = field[...].reshape(1024, 256)
        rows = lax.dot_general(left, right, (((1,), (1,)), ((), ())), preferred_element_type=jnp.float32)
        return sum_of_three(rows)

    def coefficients(h8):
        left = jnp.concatenate(three_parts(h8), axis=0)
        rows = jnp.dot(left, field[...].reshape(1024, 256), preferred_element_type=jnp.float32)
        rows = sum_of_three(rows)
        return rows[:, 0:128] - upper * half_swap(rows[:, 128:256])

    def factor(h8):
        shifted = []
        for shift in range(4):
            moved = h8 * (pltpu.roll(h8, shift, 0) if shift else h8)
            lanes = moved[:, 0:128]
            for block in range(1, 8):
                lanes = lanes + moved[:, block * 128 : (block + 1) * 128]
            dots = jnp.broadcast_to(jnp.sum(lanes, axis=1, keepdims=True), (8, 128))
            swapped = half_swap(dots)
            shifted.append((dots + swapped, dots - swapped))

        def pick(rows, at):
            return jnp.broadcast_to(rows[at : at + 1, :], (8, 128))

        low = {}
        inverse = {}
        for column in range(RANK):
            diagonal = pick(shifted[0][0], column)
            for middle in range(column):
                re, im = low[column, middle]
                diagonal = diagonal - (re * re + im * im)
            inverse[column] = lax.rsqrt(diagonal)
            for at in range(column + 1, RANK):
                distance = at - column
                re = pick(shifted[distance][0], at)
                im = pick(shifted[4 - distance][1], column)
                for middle in range(column):
                    a_re, a_im = low[at, middle]
                    b_re, b_im = low[column, middle]
                    re = re - (a_re * b_re + a_im * b_im)
                    im = im - (a_im * b_re - a_re * b_im)
                low[at, column] = (re * inverse[column], im * inverse[column])
        return low, inverse

    def solve(low, inverse, rows):
        width = rows.shape[1]
        repeat = width // 128

        def wide(value):
            return value if repeat == 1 else jnp.concatenate([value] * repeat, axis=1)

        done = []
        for at in range(RANK):
            re = jnp.broadcast_to(rows[at : at + 1, :], (8, width))
            im = jnp.broadcast_to(rows[at + 4 : at + 5, :], (8, width))
            for middle in range(at):
                l_re, l_im = low[at, middle]
                l_re, l_im = wide(l_re), wide(l_im)
                d_re, d_im = done[middle]
                re = re - (l_re * d_re - l_im * d_im)
                im = im - (l_re * d_im + l_im * d_re)
            scale = wide(inverse[at])
            done.append((re * scale, im * scale))
        at_row = lax.broadcasted_iota(jnp.int32, (8, width), 0)
        total = done[3][1]
        for at in range(RANK):
            total = jnp.where(at_row == at, done[at][0], total)
            if at < 3:
                total = jnp.where(at_row == at + 4, done[at][1], total)
        return total

    coefficient = first_in[0]
    for station in range(1, GROUP):
        coefficient = coefficient + first_in[station]

    image_copies = []
    for iteration in range(ITERS):
        image[iteration, quarter] = apply_field(coefficient)
        for at, peer in enumerate(three):
            copy = pltpu.make_async_remote_copy(
                src_ref=image.at[iteration, quarter],
                dst_ref=image.at[iteration, quarter],
                send_sem=send_image.at[iteration, at],
                recv_sem=recv_image.at[iteration, at],
                device_id=peer,
                device_id_type=MESH,
            )
            copy.start()
            image_copies.append(copy)
        for copy in image_copies[-3:]:
            copy.wait_recv()
        summed = (image[iteration, 0] + image[iteration, 1]) + (image[iteration, 2] + image[iteration, 3])
        raw = coefficients(summed)
        low, inverse = factor(summed)
        coefficient = solve(low, inverse, raw)
    basis = solve(low, inverse, summed)

    for block in range(8):
        lanes = basis[:, block * 128 : (block + 1) * 128] * upper
        basis_out[2 * block] = lanes
        basis_out[2 * block + 1] = pltpu.roll(lanes, 64, 1)

    def basis_copy(step, slot, peer):
        return pltpu.make_async_remote_copy(
            src_ref=basis_out.at[peer],
            dst_ref=basis_in.at[slot],
            send_sem=send_basis.at[step],
            recv_sem=recv_basis.at[slot],
            device_id={"station": peer},
            device_id_type=MESH,
        )

    def basis_start(step):
        peer = partner(step)

        @pl.when(peer // 8 == half)
        def _():
            basis_copy(step, mine, peer).start()

    def six(parts, which):
        return jnp.concatenate([parts[at] for at in which], axis=0)

    left = six(three_parts(basis), (0, 0, 1, 0, 1, 2))
    right = six(three_parts(turned(coefficient)), (0, 1, 0, 2, 1, 0))
    removed = lax.dot_general(left, right, (((0,), (0,)), ((), ())), preferred_element_type=jnp.float32)
    cleaned = field[...].reshape(1024, 256).astype(jnp.float32) - removed
    cleaned = cleaned.astype(jnp.bfloat16).reshape(GROUP, 2, 32, 256)
    lane_group = lax.broadcasted_iota(jnp.int32, (8, 128), 1) // 16
    compact = [jnp.zeros((8, 128), jnp.float32) for _ in range(GROUP)]
    for p in range(2):
        ours = cleaned[:, p].reshape(512, 256)
        on_real = jnp.dot(weights[0], ours, preferred_element_type=jnp.float32)
        on_imag = jnp.dot(weights[1], ours, preferred_element_type=jnp.float32)
        real_b = on_real[:, 0:128] - on_imag[:, 128:256]
        imag_b = on_real[:, 128:256] + on_imag[:, 0:128]
        squares = jnp.sum(real_b * real_b + imag_b * imag_b, axis=1, keepdims=True)
        for station in range(GROUP):
            rows = slice(station * 32, (station + 1) * 32)
            stage[station, 0, p] = real_b[rows].astype(jnp.bfloat16)
            stage[station, 1, p] = imag_b[rows].astype(jnp.bfloat16)
            for block in range(4):
                at = station * 32 + block * 8
                compact[station] = jnp.where(
                    lane_group == p * 4 + block,
                    jnp.broadcast_to(squares[at : at + 8], (8, 128)),
                    compact[station],
                )
    for station in range(GROUP):
        power_out[station] = compact[station]

    def power_copy(step, peer, slot):
        return pltpu.make_async_remote_copy(
            src_ref=power_out.at[peer],
            dst_ref=power_in.at[slot],
            send_sem=send_power.at[step],
            recv_sem=recv_power.at[slot],
            device_id={"station": peer},
            device_id_type=MESH,
        )

    def beam_copy(step, peer, slot):
        return pltpu.make_async_remote_copy(
            src_ref=stage.at[peer],
            dst_ref=arrived.at[slot],
            send_sem=send_beam.at[step],
            recv_sem=recv_beam.at[slot],
            device_id={"station": peer},
            device_id_type=MESH,
        )

    everyone(lambda step: power_copy(step, partner(step), me).start())
    everyone(lambda step: beam_copy(step, partner(step), me).start())
    power_in[me] = power_out[me]
    own_beam = pltpu.make_async_copy(stage.at[me], arrived.at[me], local_sem.at[8])
    own_beam.start()
    everyone(basis_start)

    @pl.when(me // 8 == half)
    def _():
        copy = pltpu.make_async_copy(basis_out.at[me], basis_in.at[mine], local_sem.at[9])
        copy.start()
        copy.wait()

    def power_arrive(step):
        source = partner(step)
        power_copy(step, source, source).wait_recv()

    everyone(power_arrive)
    power = power_in[0]
    for station in range(1, GROUP):
        power = power + power_in[station]
    slot = plane * 2 + core
    power_two[slot] = power
    two_copies = []
    for at, peer in enumerate(seven):
        copy = pltpu.make_async_remote_copy(
            src_ref=power_two.at[slot],
            dst_ref=power_two.at[slot],
            send_sem=send_two.at[at],
            recv_sem=recv_two.at[at],
            device_id=peer,
            device_id_type=MESH,
        )
        copy.start()
        two_copies.append(copy)

    def drain(step):
        peer = partner(step)
        x_copy(step, peer, me).wait_send()
        first_copy(step, peer, me).wait_send()
        power_copy(step, peer, me).wait_send()

        @pl.when(peer // 8 == half)
        def _():
            basis_copy(step, mine, peer).wait_send()

    everyone(drain)
    for copy in image_copies:
        copy.wait_send()

    for copy in two_copies:
        copy.wait_recv()
    power = power_two[0]
    for at in range(1, 8):
        power = power + power_two[at]
    rescale[...] = lax.rsqrt(power / (CHANNELS * TIME) + 1e-06)

    for c in range(8):

        @pl.when(2 * c + me // 8 != me)
        def _():
            basis_copy(0, c, 2 * c + me // 8).wait_recv()

    def beam_arrive(step):
        source = partner(step)
        beam_copy(step, source, source).wait_recv()
        beam_copy(step, source, me).wait_send()

    everyone(beam_arrive)
    own_beam.wait()
    for copy in two_copies:
        copy.wait_send()


def normalise(arrived, rescale, basis, out, sub_hbm, result, sub, sem):
    scales = []
    for p in range(2):
        rows = []
        for block in range(4):
            lane = (p * 4 + block) * 16
            rows.append(jnp.broadcast_to(rescale[:, lane : lane + 1], (8, 128)))
        scales.append(jnp.concatenate(rows, axis=0))
    copies = []
    for c in range(8):
        for side in range(2):
            for part in range(2):
                for p in range(2):
                    value = arrived[2 * c + side, part, p].astype(jnp.float32) * scales[p]
                    result[part, c, p, :, side * 128 : (side + 1) * 128] = value.astype(jnp.bfloat16)
        copy = pltpu.make_async_copy(result.at[:, c], out.at[:, c], sem.at[c])
        copy.start()
        copies.append(copy)
    for c in range(8):
        for p in range(2):
            for part in range(2):
                at = part * 4
                sub[part, c, pl.ds(p, 4, stride=2), :] = basis[c, at : at + 4, p * 32 : (p + 1) * 32]
    copy = pltpu.make_async_copy(sub, sub_hbm, sem.at[8])
    copy.start()
    copies.append(copy)
    for copy in copies:
        copy.wait()


def body(voltages, start_seed, beam_phase, station_delay):
    vmem = pl.BlockSpec(memory_space=pltpu.VMEM)
    hbm = pl.BlockSpec(memory_space=pltpu.MemorySpace.HBM)
    anywhere = pl.BlockSpec(memory_space=pl.ANY)
    dma = pltpu.SemaphoreType.DMA
    f32, bf16 = jnp.float32, jnp.bfloat16
    def kept(value):
        return pltpu.with_memory_space_constraint(value, pltpu.MemorySpace.HBM)

    operands = (
        voltages,
        start_seed.reshape(2, 8, 8, 32),
        beam_phase,
        station_delay.reshape(1, STATIONS),
    )
    arrived, rescale, basis = pl.pallas_call(
        exchange,
        out_shape=(
            jax.ShapeDtypeStruct((16, 2, 2, 32, 128), bf16),
            jax.ShapeDtypeStruct((8, 128), f32),
            jax.ShapeDtypeStruct((8, 8, 128), f32),
        ),
        in_specs=[hbm] * 4,
        out_specs=(vmem, vmem, vmem),
        scratch_shapes=[
            pltpu.VMEM((8, 2, 2, 32, 256), bf16),
            pltpu.VMEM((2, 8, 8, 32), jnp.int32),
            pltpu.VMEM((512, 512), jnp.int32),
            pltpu.VMEM((1, 512), jnp.int32),
            pltpu.VMEM((GROUP, 2, 32, 256), bf16),
            pltpu.VMEM((GROUP, 8, 128), f32),
            pltpu.VMEM((GROUP, 8, 128), f32),
            pltpu.VMEM((ITERS, QUARTERS, 8, 1024), f32),
            pltpu.VMEM((2, 512, 512), bf16),
            pltpu.VMEM((GROUP, 2, 2, 32, 128), bf16),
            pltpu.VMEM((GROUP, 8, 128), f32),
            pltpu.VMEM((GROUP, 8, 128), f32),
            pltpu.VMEM((8, 8, 128), f32),
            pltpu.VMEM((GROUP, 8, 128), f32),
            dma((10,)),
            dma((16,)),
            dma((16,)),
            dma((16,)),
            dma((16,)),
            dma((ITERS, 3)),
            dma((ITERS, 3)),
            dma((16,)),
            dma((8,)),
            dma((16,)),
            dma((16,)),
            dma((7,)),
            dma((7,)),
            dma((16,)),
            dma((16,)),
        ],
        compiler_params=pltpu.CompilerParams(
            collective_id=0, has_side_effects=True, vmem_limit_bytes=40 * 1024 * 1024
        ),
    )(*map(kept, operands))
    beam_output, subspace = pl.pallas_call(
        normalise,
        out_shape=(
            jax.ShapeDtypeStruct((2, 8, 2, 32, 256), bf16),
            jax.ShapeDtypeStruct((2, 8, 8, 32), f32),
        ),
        in_specs=[vmem] * 3,
        out_specs=(anywhere, anywhere),
        scratch_shapes=[
            pltpu.VMEM((2, 8, 2, 32, 256), bf16),
            pltpu.VMEM((2, 8, 8, 32), f32),
            dma((9,)),
        ],
        compiler_params=pltpu.CompilerParams(vmem_limit_bytes=40 * 1024 * 1024),
    )(arrived, rescale, basis)
    return beam_output, subspace.reshape(2, 8, 4, 2, 32)


def solution(mesh):
    in_specs = (
        P(None, "channel", None, "station", "tm"),
        P(None, "channel", None, None, "station"),
        P(),
        P(),
    )
    out_specs = (
        P(None, "channel", None, "station", "tm"),
        P(None, "channel", None, None, "station"),
    )
    return jax.shard_map(body, mesh=mesh, in_specs=in_specs, out_specs=out_specs, check_vma=False)
```

```python
import functools

import jax
import jax.numpy as jnp
from jax import lax
from jax.experimental import pallas as pl
from jax.experimental.pallas import tpu as pltpu
from jax.sharding import PartitionSpec as P

STATIONS = 512
CHANNELS = 32
ITERS = 3
PHASES = 1024
TIME = 512
RANK = 4
GROUP = 16
QUARTERS = 4

MESH = pl.DeviceIdType.MESH

COS_TERMS = (
    0.9999999998855527,
    -4.934802185863431,
    4.058711817242859,
    -1.3352602861671086,
    0.23532082553812417,
    -0.025785808775470303,
    0.0019043289643584185,
    -8.86909374720357e-05,
)
SIN_TERMS = (
    3.141592653568331,
    -5.167712777297557,
    2.5501639819324518,
    -0.599264064211247,
    0.0821440508162118,
    -0.007366486943808629,
    0.000461586777512204,
    -1.8944663042615234e-05,
)


FARTHEST_FIRST = (
    (2, 2),
    (2, 1),
    (2, 3),
    (1, 2),
    (3, 2),
    (1, 1),
    (3, 3),
    (1, 3),
    (3, 1),
    (2, 0),
    (0, 2),
    (1, 0),
    (3, 0),
    (0, 1),
    (0, 3),
)


def horner(terms, scale, v):
    total = jnp.full_like(v, terms[-1] * scale)
    for term in terms[-2::-1]:
        total = total * v + jnp.float32(term * scale)
    return total


def three_parts(value):
    high = value.astype(jnp.bfloat16)
    rest = value - high.astype(jnp.float32)
    middle = rest.astype(jnp.bfloat16)
    low = (rest - middle.astype(jnp.float32)).astype(jnp.bfloat16)
    return high, middle, low


def sum_of_three(rows):
    return rows[0:8] + (rows[8:16] + rows[16:24])


def half_swap(rows):
    return pltpu.roll(rows, 4, 0)


def exchange(
    volt,
    seed_hbm,
    phase,
    delay_hbm,
    arrived,
    rescale,
    basis_in,
    local_x,
    seed,
    phases,
    delay,
    field,
    first_out,
    first_in,
    image,
    weights,
    stage,
    power_out,
    power_in,
    power_two,
    basis_out,
    local_sem,
    send_x,
    recv_x,
    send_first,
    recv_first,
    send_image,
    recv_image,
    send_basis,
    recv_basis,
    send_power,
    recv_power,
    send_two,
    recv_two,
    send_beam,
    recv_beam,
):
    core = lax.axis_index("tm")
    me = lax.axis_index("station")
    plane = lax.axis_index("channel")
    mine = me // 2
    half = me % 2
    twin = me + 1 - 2 * half
    quarter = core * 2 + half

    others = []
    for across, along in FARTHEST_FIRST:
        row = (me // 4 + across) % 4
        column = (me % 4 + along) % 4
        others.append(row * 4 + column)

    def everyone(start):
        for peer in others:
            start(peer)

    def together(buffer, sem):
        part = buffer.at[pl.ds(0, GROUP - 1)]
        return pltpu.make_async_copy(part, part, sem)

    loads = [
        pltpu.make_async_copy(
            volt.at[part, :, :, :, pl.ds(side * 128, 128)],
            local_x.at[:, side, :, :, pl.ds(part * 128, 128)],
            local_sem.at[part * 2 + side],
        )
        for part in range(2)
        for side in range(2)
    ]
    loads.append(pltpu.make_async_copy(seed_hbm, seed, local_sem.at[4]))
    loads.append(pltpu.make_async_copy(phase, phases, local_sem.at[5]))
    loads.append(pltpu.make_async_copy(delay_hbm, delay, local_sem.at[6]))

    barrier = pltpu.get_barrier_semaphore()
    three = (
        {"tm": 1 - core, "station": twin},
        {"station": twin},
        {"tm": 1 - core},
    )
    seven = [{"channel": (plane + 2) % 4}, {"tm": 1 - core, "channel": (plane + 2) % 4}]
    for step in (1, 3):
        other = (plane + step) % 4
        seven.append({"channel": other})
        seven.append({"tm": 1 - core, "channel": other})
    seven.append({"tm": 1 - core})

    def greet(peer):
        pl.semaphore_signal(barrier, inc=1, device_id=peer, device_id_type=MESH)

    everyone(lambda peer: greet({"station": peer}))
    for peer in seven:
        greet(peer)
    greet(three[0])
    for load in loads:
        load.start()
    row = lax.broadcasted_iota(jnp.int32, (8, 128), 0)
    upper = jnp.where(row < 4, 1.0, -1.0).astype(jnp.float32)

    for load in loads[:5]:
        load.wait()
    for c in range(8):
        left = []
        for p in range(2):
            real_s = seed[0, c, pl.ds(p, 4, stride=2), :].astype(jnp.float32)
            imag_s = seed[1, c, pl.ds(p, 4, stride=2), :].astype(jnp.float32)
            left.append(jnp.concatenate([real_s, imag_s], axis=0))
        left = jnp.concatenate(left, axis=1).astype(jnp.bfloat16)
        for side in range(2):
            right = local_x[c, side].reshape(64, 256)
            rows = jnp.dot(left, right, preferred_element_type=jnp.float32)
            first_out[2 * c + side] = half_swap(rows[:, 128:256]) + upper * rows[:, 0:128]

    pl.semaphore_wait(barrier, GROUP - 1 + len(seven) + 1)

    def first_copy(peer):
        return pltpu.make_async_remote_copy(
            src_ref=first_out.at[peer],
            dst_ref=first_in.at[me],
            send_sem=send_first,
            recv_sem=recv_first,
            device_id={"station": peer},
            device_id_type=MESH,
        )

    everyone(lambda peer: first_copy(peer).start())
    def x_copy(peer):
        return pltpu.make_async_remote_copy(
            src_ref=local_x.at[peer // 2, peer % 2],
            dst_ref=field.at[me],
            send_sem=send_x,
            recv_sem=recv_x,
            device_id={"station": peer},
            device_id_type=MESH,
        )

    everyone(lambda peer: x_copy(peer).start())
    own_x = pltpu.make_async_copy(local_x.at[mine, half], field.at[me], local_sem.at[7])
    own_x.start()
    first_in[me] = first_out[me]

    loads[5].wait()
    loads[6].wait()
    number = plane * 8 + mine + 1
    norming = STATIONS**-0.5

    def weight_rows(block, carry):
        rows = pl.ds(pl.multiple_of(block * 32, 32), 32)
        index = (phases[rows, :] + delay[...]) * number
        wrapped = (index + PHASES // 2) & (PHASES - 1)
        u = (wrapped - PHASES // 2).astype(jnp.float32) * jnp.float32(2.0 / PHASES)
        v = u * u
        weights[0, rows, :] = horner(COS_TERMS, norming, v).astype(jnp.bfloat16)
        weights[1, rows, :] = (u * horner(SIN_TERMS, -norming, v)).astype(jnp.bfloat16)
        return carry

    lax.fori_loop(0, 16, weight_rows, 0)

    together(first_in, recv_first).wait()
    together(field, recv_x).wait()
    own_x.wait()

    def turned(c8):
        return jnp.concatenate([c8, half_swap(c8) * upper], axis=1)

    def apply_field(c8):
        left = jnp.concatenate(three_parts(turned(c8)), axis=0)
        right = field[...].reshape(1024, 256)
        rows = lax.dot_general(left, right, (((1,), (1,)), ((), ())), preferred_element_type=jnp.float32)
        return sum_of_three(rows)

    def coefficients(h8):
        left = jnp.concatenate(three_parts(h8), axis=0)
        rows = jnp.dot(left, field[...].reshape(1024, 256), preferred_element_type=jnp.float32)
        rows = sum_of_three(rows)
        return rows[:, 0:128] - upper * half_swap(rows[:, 128:256])

    def factor(h8):
        shifted = []
        for shift in range(4):
            moved = h8 * (pltpu.roll(h8, shift, 0) if shift else h8)
            lanes = moved[:, 0:128]
            for block in range(1, 8):
                lanes = lanes + moved[:, block * 128 : (block + 1) * 128]
            dots = jnp.broadcast_to(jnp.sum(lanes, axis=1, keepdims=True), (8, 128))
            swapped = half_swap(dots)
            shifted.append((dots + swapped, dots - swapped))

        def pick(rows, at):
            return jnp.broadcast_to(rows[at : at + 1, :], (8, 128))

        low = {}
        inverse = {}
        for column in range(RANK):
            diagonal = pick(shifted[0][0], column)
            for middle in range(column):
                re, im = low[column, middle]
                diagonal = diagonal - (re * re + im * im)
            inverse[column] = lax.rsqrt(diagonal)
            for at in range(column + 1, RANK):
                distance = at - column
                re = pick(shifted[distance][0], at)
                im = pick(shifted[4 - distance][1], column)
                for middle in range(column):
                    a_re, a_im = low[at, middle]
                    b_re, b_im = low[column, middle]
                    re = re - (a_re * b_re + a_im * b_im)
                    im = im - (a_im * b_re - a_re * b_im)
                low[at, column] = (re * inverse[column], im * inverse[column])
        return low, inverse

    def solve(low, inverse, rows):
        width = rows.shape[1]
        repeat = width // 128

        def wide(value):
            return value if repeat == 1 else jnp.concatenate([value] * repeat, axis=1)

        done = []
        for at in range(RANK):
            re = jnp.broadcast_to(rows[at : at + 1, :], (8, width))
            im = jnp.broadcast_to(rows[at + 4 : at + 5, :], (8, width))
            for middle in range(at):
                l_re, l_im = low[at, middle]
                l_re, l_im = wide(l_re), wide(l_im)
                d_re, d_im = done[middle]
                re = re - (l_re * d_re - l_im * d_im)
                im = im - (l_re * d_im + l_im * d_re)
            scale = wide(inverse[at])
            done.append((re * scale, im * scale))
        at_row = lax.broadcasted_iota(jnp.int32, (8, width), 0)
        total = done[3][1]
        for at in range(RANK):
            total = jnp.where(at_row == at, done[at][0], total)
            if at < 3:
                total = jnp.where(at_row == at + 4, done[at][1], total)
        return total

    coefficient = first_in[0]
    for station in range(1, GROUP):
        coefficient = coefficient + first_in[station]

    image_copies = []
    for iteration in range(ITERS):
        image[iteration, quarter] = apply_field(coefficient)
        for at, peer in enumerate(three):
            copy = pltpu.make_async_remote_copy(
                src_ref=image.at[iteration, quarter],
                dst_ref=image.at[iteration, quarter],
                send_sem=send_image.at[iteration, at],
                recv_sem=recv_image.at[iteration, at],
                device_id=peer,
                device_id_type=MESH,
            )
            copy.start()
            image_copies.append(copy)
        for copy in image_copies[-3:]:
            copy.wait_recv()
        summed = (image[iteration, 0] + image[iteration, 1]) + (image[iteration, 2] + image[iteration, 3])
        raw = coefficients(summed)
        low, inverse = factor(summed)
        coefficient = solve(low, inverse, raw)
    basis = solve(low, inverse, summed)

    for block in range(8):
        lanes = basis[:, block * 128 : (block + 1) * 128] * upper
        basis_out[2 * block] = lanes
        basis_out[2 * block + 1] = pltpu.roll(lanes, 64, 1)

    def basis_copy(peer, slot):
        return pltpu.make_async_remote_copy(
            src_ref=basis_out.at[peer],
            dst_ref=basis_in.at[slot],
            send_sem=send_basis.at[peer],
            recv_sem=recv_basis.at[slot],
            device_id={"station": peer},
            device_id_type=MESH,
        )

    def served(start):
        for inner in range(8):
            peer = half * 8 + inner

            @pl.when(peer != me)
            def _():
                start(basis_copy(peer, mine))

    def six(parts, which):
        return jnp.concatenate([parts[at] for at in which], axis=0)

    left = six(three_parts(basis), (0, 0, 1, 0, 1, 2))
    right = six(three_parts(turned(coefficient)), (0, 1, 0, 2, 1, 0))
    removed = lax.dot_general(left, right, (((0,), (0,)), ((), ())), preferred_element_type=jnp.float32)
    cleaned = field[...].reshape(1024, 256).astype(jnp.float32) - removed
    cleaned = cleaned.astype(jnp.bfloat16).reshape(GROUP, 2, 32, 256)
    lane_group = lax.broadcasted_iota(jnp.int32, (8, 128), 1) // 16
    compact = [jnp.zeros((8, 128), jnp.float32) for _ in range(GROUP)]
    for p in range(2):
        ours = cleaned[:, p].reshape(512, 256)
        on_real = jnp.dot(weights[0], ours, preferred_element_type=jnp.float32)
        on_imag = jnp.dot(weights[1], ours, preferred_element_type=jnp.float32)
        real_b = on_real[:, 0:128] - on_imag[:, 128:256]
        imag_b = on_real[:, 128:256] + on_imag[:, 0:128]
        squares = jnp.sum(real_b * real_b + imag_b * imag_b, axis=1, keepdims=True)
        for station in range(GROUP):
            rows = slice(station * 32, (station + 1) * 32)
            stage[station, 0, p] = real_b[rows].astype(jnp.bfloat16)
            stage[station, 1, p] = imag_b[rows].astype(jnp.bfloat16)
            for block in range(4):
                at = station * 32 + block * 8
                compact[station] = jnp.where(
                    lane_group == p * 4 + block,
                    jnp.broadcast_to(squares[at : at + 8], (8, 128)),
                    compact[station],
                )
    for station in range(GROUP):
        power_out[station] = compact[station]

    def power_copy(peer):
        return pltpu.make_async_remote_copy(
            src_ref=power_out.at[peer],
            dst_ref=power_in.at[me],
            send_sem=send_power,
            recv_sem=recv_power,
            device_id={"station": peer},
            device_id_type=MESH,
        )

    def beam_copy(peer):
        return pltpu.make_async_remote_copy(
            src_ref=stage.at[peer],
            dst_ref=arrived.at[me],
            send_sem=send_beam,
            recv_sem=recv_beam,
            device_id={"station": peer},
            device_id_type=MESH,
        )

    everyone(lambda peer: power_copy(peer).start())
    everyone(lambda peer: beam_copy(peer).start())
    power_in[me] = power_out[me]
    own_beam = pltpu.make_async_copy(stage.at[me], arrived.at[me], local_sem.at[8])
    own_beam.start()
    served(lambda copy: copy.start())

    @pl.when(me // 8 == half)
    def _():
        copy = pltpu.make_async_copy(basis_out.at[me], basis_in.at[mine], local_sem.at[9])
        copy.start()
        copy.wait()

    together(power_in, recv_power).wait()
    power = power_in[0]
    for station in range(1, GROUP):
        power = power + power_in[station]
    slot = plane * 2 + core
    power_two[slot] = power
    two_copies = []
    for at, peer in enumerate(seven):
        copy = pltpu.make_async_remote_copy(
            src_ref=power_two.at[slot],
            dst_ref=power_two.at[slot],
            send_sem=send_two.at[at],
            recv_sem=recv_two.at[at],
            device_id=peer,
            device_id_type=MESH,
        )
        copy.start()
        two_copies.append(copy)

    together(first_out, send_first).wait()
    together(field, send_x).wait()
    together(power_out, send_power).wait()
    for copy in image_copies:
        copy.wait_send()
    served(lambda copy: copy.wait_send())
    for c in range(8):

        @pl.when(2 * c + me // 8 != me)
        def _():
            basis_copy(2 * c + me // 8, c).wait_recv()

    together(stage, send_beam).wait()
    together(arrived, recv_beam).wait()
    own_beam.wait()

    for copy in two_copies:
        copy.wait_recv()
    power = power_two[0]
    for at in range(1, 8):
        power = power + power_two[at]
    rescale[...] = lax.rsqrt(power / (CHANNELS * TIME) + 1e-06)

    for copy in two_copies:
        copy.wait_send()


def normalise(arrived, rescale, basis, out, sub_hbm, result, sub, sem):
    scales = []
    for p in range(2):
        rows = []
        for block in range(4):
            lane = (p * 4 + block) * 16
            rows.append(jnp.broadcast_to(rescale[:, lane : lane + 1], (8, 128)))
        scales.append(jnp.concatenate(rows, axis=0))
    copies = []
    for c in range(8):
        for side in range(2):
            for part in range(2):
                for p in range(2):
                    value = arrived[2 * c + side, part, p].astype(jnp.float32) * scales[p]
                    result[part, c, p, :, side * 128 : (side + 1) * 128] = value.astype(jnp.bfloat16)
        copy = pltpu.make_async_copy(result.at[:, c], out.at[:, c], sem.at[c])
        copy.start()
        copies.append(copy)
    for c in range(8):
        for p in range(2):
            for part in range(2):
                at = part * 4
                sub[part, c, pl.ds(p, 4, stride=2), :] = basis[c, at : at + 4, p * 32 : (p + 1) * 32]
    copy = pltpu.make_async_copy(sub, sub_hbm, sem.at[8])
    copy.start()
    copies.append(copy)
    for copy in copies:
        copy.wait()


def body(voltages, start_seed, beam_phase, station_delay):
    vmem = pl.BlockSpec(memory_space=pltpu.VMEM)
    hbm = pl.BlockSpec(memory_space=pltpu.MemorySpace.HBM)
    anywhere = pl.BlockSpec(memory_space=pl.ANY)
    dma = pltpu.SemaphoreType.DMA
    f32, bf16 = jnp.float32, jnp.bfloat16
    def kept(value):
        return pltpu.with_memory_space_constraint(value, pltpu.MemorySpace.HBM)

    operands = (
        voltages,
        start_seed.reshape(2, 8, 8, 32),
        beam_phase,
        station_delay.reshape(1, STATIONS),
    )
    arrived, rescale, basis = pl.pallas_call(
        exchange,
        out_shape=(
            jax.ShapeDtypeStruct((16, 2, 2, 32, 128), bf16),
            jax.ShapeDtypeStruct((8, 128), f32),
            jax.ShapeDtypeStruct((8, 8, 128), f32),
        ),
        in_specs=[hbm] * 4,
        out_specs=(vmem, vmem, vmem),
        scratch_shapes=[
            pltpu.VMEM((8, 2, 2, 32, 256), bf16),
            pltpu.VMEM((2, 8, 8, 32), jnp.int32),
            pltpu.VMEM((512, 512), jnp.int32),
            pltpu.VMEM((1, 512), jnp.int32),
            pltpu.VMEM((GROUP, 2, 32, 256), bf16),
            pltpu.VMEM((GROUP, 8, 128), f32),
            pltpu.VMEM((GROUP, 8, 128), f32),
            pltpu.VMEM((ITERS, QUARTERS, 8, 1024), f32),
            pltpu.VMEM((2, 512, 512), bf16),
            pltpu.VMEM((GROUP, 2, 2, 32, 128), bf16),
            pltpu.VMEM((GROUP, 8, 128), f32),
            pltpu.VMEM((GROUP, 8, 128), f32),
            pltpu.VMEM((8, 8, 128), f32),
            pltpu.VMEM((GROUP, 8, 128), f32),
            dma((10,)),
            dma(()),
            dma(()),
            dma(()),
            dma(()),
            dma((ITERS, 3)),
            dma((ITERS, 3)),
            dma((16,)),
            dma((8,)),
            dma(()),
            dma(()),
            dma((7,)),
            dma((7,)),
            dma(()),
            dma(()),
        ],
        compiler_params=pltpu.CompilerParams(
            collective_id=0, has_side_effects=True, vmem_limit_bytes=40 * 1024 * 1024
        ),
    )(*map(kept, operands))
    beam_output, subspace = pl.pallas_call(
        normalise,
        out_shape=(
            jax.ShapeDtypeStruct((2, 8, 2, 32, 256), bf16),
            jax.ShapeDtypeStruct((2, 8, 8, 32), f32),
        ),
        in_specs=[vmem] * 3,
        out_specs=(anywhere, anywhere),
        scratch_shapes=[
            pltpu.VMEM((2, 8, 2, 32, 256), bf16),
            pltpu.VMEM((2, 8, 8, 32), f32),
            dma((9,)),
        ],
        compiler_params=pltpu.CompilerParams(vmem_limit_bytes=40 * 1024 * 1024),
    )(arrived, rescale, basis)
    return beam_output, subspace.reshape(2, 8, 4, 2, 32)


def solution(mesh):
    in_specs = (
        P(None, "channel", None, "station", "tm"),
        P(None, "channel", None, None, "station"),
        P(),
        P(),
    )
    out_specs = (
        P(None, "channel", None, "station", "tm"),
        P(None, "channel", None, None, "station"),
    )
    return jax.shard_map(body, mesh=mesh, in_specs=in_specs, out_specs=out_specs, check_vma=False)
```

```python
import functools

import jax
import jax.numpy as jnp
from jax import lax
from jax.experimental import pallas as pl
from jax.experimental.pallas import tpu as pltpu
from jax.sharding import PartitionSpec as P

STATIONS = 512
CHANNELS = 32
ITERS = 3
PHASES = 1024
TIME = 512
RANK = 4
GROUP = 16
QUARTERS = 4

MESH = pl.DeviceIdType.MESH

COS_TERMS = (
    0.9999999998855527,
    -4.934802185863431,
    4.058711817242859,
    -1.3352602861671086,
    0.23532082553812417,
    -0.025785808775470303,
    0.0019043289643584185,
    -8.86909374720357e-05,
)
SIN_TERMS = (
    3.141592653568331,
    -5.167712777297557,
    2.5501639819324518,
    -0.599264064211247,
    0.0821440508162118,
    -0.007366486943808629,
    0.000461586777512204,
    -1.8944663042615234e-05,
)


FARTHEST_FIRST = (
    (2, 2),
    (2, 1),
    (2, 3),
    (1, 2),
    (3, 2),
    (1, 1),
    (3, 3),
    (1, 3),
    (3, 1),
    (2, 0),
    (0, 2),
    (1, 0),
    (3, 0),
    (0, 1),
    (0, 3),
)
BEAM_TURNS = (0, 13, 1, 12, 2, 11, 3, 14, 4, 9, 10, 5, 6, 7, 8)


def horner(terms, scale, v):
    total = jnp.full_like(v, terms[-1] * scale)
    for term in terms[-2::-1]:
        total = total * v + jnp.float32(term * scale)
    return total


def three_parts(value):
    high = value.astype(jnp.bfloat16)
    rest = value - high.astype(jnp.float32)
    middle = rest.astype(jnp.bfloat16)
    low = (rest - middle.astype(jnp.float32)).astype(jnp.bfloat16)
    return high, middle, low


def sum_of_three(rows):
    return rows[0:8] + (rows[8:16] + rows[16:24])


def half_swap(rows):
    return pltpu.roll(rows, 4, 0)


def exchange(
    volt,
    seed_hbm,
    phase,
    delay_hbm,
    arrived,
    rescale,
    power_in,
    local_x,
    seed,
    phases,
    delay,
    field,
    first_out,
    first_in,
    image,
    weights,
    stage,
    power_out,
    power_two,
    local_sem,
    send_x,
    recv_x,
    send_first,
    recv_first,
    send_image,
    recv_image,
    send_power,
    recv_power,
    send_two,
    recv_two,
    send_beam,
    recv_beam,
):
    core = lax.axis_index("tm")
    me = lax.axis_index("station")
    plane = lax.axis_index("channel")
    mine = me // 2
    half = me % 2
    twin = me + 1 - 2 * half
    quarter = core * 2 + half

    others = []
    for across, along in FARTHEST_FIRST:
        row = (me // 4 + across) % 4
        column = (me % 4 + along) % 4
        others.append(row * 4 + column)

    def everyone(start):
        for peer in others:
            start(peer)

    def together(buffer, sem):
        part = buffer.at[pl.ds(0, GROUP - 1)]
        return pltpu.make_async_copy(part, part, sem)

    loads = [
        pltpu.make_async_copy(
            volt.at[part, :, :, :, pl.ds(side * 128, 128)],
            local_x.at[:, side, :, :, pl.ds(part * 128, 128)],
            local_sem.at[part * 2 + side],
        )
        for part in range(2)
        for side in range(2)
    ]
    loads.append(pltpu.make_async_copy(seed_hbm, seed, local_sem.at[4]))
    loads.append(pltpu.make_async_copy(phase, phases, local_sem.at[5]))
    loads.append(pltpu.make_async_copy(delay_hbm, delay, local_sem.at[6]))

    barrier = pltpu.get_barrier_semaphore()
    three = (
        {"tm": 1 - core, "station": twin},
        {"station": twin},
        {"tm": 1 - core},
    )
    seven = [{"channel": (plane + 2) % 4}, {"tm": 1 - core, "channel": (plane + 2) % 4}]
    for step in (1, 3):
        other = (plane + step) % 4
        seven.append({"channel": other})
        seven.append({"tm": 1 - core, "channel": other})
    seven.append({"tm": 1 - core})

    def greet(peer):
        pl.semaphore_signal(barrier, inc=1, device_id=peer, device_id_type=MESH)

    everyone(lambda peer: greet({"station": peer}))
    for peer in seven:
        greet(peer)
    greet(three[0])
    for load in loads:
        load.start()
    row = lax.broadcasted_iota(jnp.int32, (8, 128), 0)
    upper = jnp.where(row < 4, 1.0, -1.0).astype(jnp.float32)

    for load in loads[:5]:
        load.wait()
    for c in range(8):
        left = []
        for p in range(2):
            real_s = seed[0, c, pl.ds(p, 4, stride=2), :].astype(jnp.float32)
            imag_s = seed[1, c, pl.ds(p, 4, stride=2), :].astype(jnp.float32)
            left.append(jnp.concatenate([real_s, imag_s], axis=0))
        left = jnp.concatenate(left, axis=1).astype(jnp.bfloat16)
        for side in range(2):
            right = local_x[c, side].reshape(64, 256)
            rows = jnp.dot(left, right, preferred_element_type=jnp.float32)
            first_out[2 * c + side] = half_swap(rows[:, 128:256]) + upper * rows[:, 0:128]

    pl.semaphore_wait(barrier, GROUP - 1 + len(seven) + 1)

    def first_copy(peer):
        return pltpu.make_async_remote_copy(
            src_ref=first_out.at[peer],
            dst_ref=first_in.at[me],
            send_sem=send_first,
            recv_sem=recv_first,
            device_id={"station": peer},
            device_id_type=MESH,
        )

    everyone(lambda peer: first_copy(peer).start())
    def x_copy(peer):
        return pltpu.make_async_remote_copy(
            src_ref=local_x.at[peer // 2, peer % 2],
            dst_ref=field.at[me],
            send_sem=send_x,
            recv_sem=recv_x,
            device_id={"station": peer},
            device_id_type=MESH,
        )

    everyone(lambda peer: x_copy(peer).start())
    own_x = pltpu.make_async_copy(local_x.at[mine, half], field.at[me], local_sem.at[7])
    own_x.start()
    first_in[me] = first_out[me]

    loads[5].wait()
    loads[6].wait()
    number = plane * 8 + mine + 1
    norming = STATIONS**-0.5

    def weight_rows(block, carry):
        rows = pl.ds(pl.multiple_of(block * 32, 32), 32)
        index = (phases[rows, :] + delay[...]) * number
        wrapped = (index + PHASES // 2) & (PHASES - 1)
        u = (wrapped - PHASES // 2).astype(jnp.float32) * jnp.float32(2.0 / PHASES)
        v = u * u
        weights[0, rows, :] = horner(COS_TERMS, norming, v).astype(jnp.bfloat16)
        weights[1, rows, :] = (u * horner(SIN_TERMS, -norming, v)).astype(jnp.bfloat16)
        return carry

    lax.fori_loop(0, 16, weight_rows, 0)

    together(first_in, recv_first).wait()
    together(field, recv_x).wait()
    own_x.wait()

    def turned(c8):
        return jnp.concatenate([c8, half_swap(c8) * upper], axis=1)

    def apply_field(c8):
        left = jnp.concatenate(three_parts(turned(c8)), axis=0)
        right = field[...].reshape(1024, 256)
        rows = lax.dot_general(left, right, (((1,), (1,)), ((), ())), preferred_element_type=jnp.float32)
        return sum_of_three(rows)

    def coefficients(h8):
        left = jnp.concatenate(three_parts(h8), axis=0)
        rows = jnp.dot(left, field[...].reshape(1024, 256), preferred_element_type=jnp.float32)
        rows = sum_of_three(rows)
        return rows[:, 0:128] - upper * half_swap(rows[:, 128:256])

    def factor(h8):
        shifted = []
        for shift in range(4):
            moved = h8 * (pltpu.roll(h8, shift, 0) if shift else h8)
            lanes = moved[:, 0:128]
            for block in range(1, 8):
                lanes = lanes + moved[:, block * 128 : (block + 1) * 128]
            dots = jnp.broadcast_to(jnp.sum(lanes, axis=1, keepdims=True), (8, 128))
            swapped = half_swap(dots)
            shifted.append((dots + swapped, dots - swapped))

        def pick(rows, at):
            return jnp.broadcast_to(rows[at : at + 1, :], (8, 128))

        low = {}
        inverse = {}
        for column in range(RANK):
            diagonal = pick(shifted[0][0], column)
            for middle in range(column):
                re, im = low[column, middle]
                diagonal = diagonal - (re * re + im * im)
            inverse[column] = lax.rsqrt(diagonal)
            for at in range(column + 1, RANK):
                distance = at - column
                re = pick(shifted[distance][0], at)
                im = pick(shifted[4 - distance][1], column)
                for middle in range(column):
                    a_re, a_im = low[at, middle]
                    b_re, b_im = low[column, middle]
                    re = re - (a_re * b_re + a_im * b_im)
                    im = im - (a_im * b_re - a_re * b_im)
                low[at, column] = (re * inverse[column], im * inverse[column])
        return low, inverse

    def solve(low, inverse, rows):
        width = rows.shape[1]
        repeat = width // 128

        def wide(value):
            return value if repeat == 1 else jnp.concatenate([value] * repeat, axis=1)

        done = []
        for at in range(RANK):
            re = jnp.broadcast_to(rows[at : at + 1, :], (8, width))
            im = jnp.broadcast_to(rows[at + 4 : at + 5, :], (8, width))
            for middle in range(at):
                l_re, l_im = low[at, middle]
                l_re, l_im = wide(l_re), wide(l_im)
                d_re, d_im = done[middle]
                re = re - (l_re * d_re - l_im * d_im)
                im = im - (l_re * d_im + l_im * d_re)
            scale = wide(inverse[at])
            done.append((re * scale, im * scale))
        at_row = lax.broadcasted_iota(jnp.int32, (8, width), 0)
        total = done[3][1]
        for at in range(RANK):
            total = jnp.where(at_row == at, done[at][0], total)
            if at < 3:
                total = jnp.where(at_row == at + 4, done[at][1], total)
        return total

    coefficient = first_in[0]
    for station in range(1, GROUP):
        coefficient = coefficient + first_in[station]

    image_copies = []
    for iteration in range(ITERS):
        image[iteration, quarter] = apply_field(coefficient)
        for at, peer in enumerate(three):
            copy = pltpu.make_async_remote_copy(
                src_ref=image.at[iteration, quarter],
                dst_ref=image.at[iteration, quarter],
                send_sem=send_image.at[iteration, at],
                recv_sem=recv_image.at[iteration, at],
                device_id=peer,
                device_id_type=MESH,
            )
            copy.start()
            image_copies.append(copy)
        for copy in image_copies[-3:]:
            copy.wait_recv()
        summed = (image[iteration, 0] + image[iteration, 1]) + (image[iteration, 2] + image[iteration, 3])
        raw = coefficients(summed)
        low, inverse = factor(summed)
        coefficient = solve(low, inverse, raw)
    basis = solve(low, inverse, summed)

    def six(parts, which):
        return jnp.concatenate([parts[at] for at in which], axis=0)

    left = six(three_parts(basis), (0, 0, 1, 0, 1, 2))
    right = six(three_parts(turned(coefficient)), (0, 1, 0, 2, 1, 0))
    removed = lax.dot_general(left, right, (((0,), (0,)), ((), ())), preferred_element_type=jnp.float32)
    cleaned = field[...].reshape(1024, 256).astype(jnp.float32) - removed
    cleaned = cleaned.astype(jnp.bfloat16).reshape(GROUP, 2, 32, 256)
    lane_group = lax.broadcasted_iota(jnp.int32, (8, 128), 1) // 8
    compact = []
    for block in range(8):
        lanes = basis[:, block * 128 : (block + 1) * 128] * upper
        compact += [pltpu.roll(lanes, 64, 1), lanes]
    for p in range(2):
        ours = cleaned[:, p].reshape(512, 256)
        on_real = jnp.dot(weights[0], ours, preferred_element_type=jnp.float32)
        on_imag = jnp.dot(weights[1], ours, preferred_element_type=jnp.float32)
        real_b = on_real[:, 0:128] - on_imag[:, 128:256]
        imag_b = on_real[:, 128:256] + on_imag[:, 0:128]
        squares = jnp.sum(real_b * real_b + imag_b * imag_b, axis=1, keepdims=True)
        for station in range(GROUP):
            rows = slice(station * 32, (station + 1) * 32)
            stage[station, 0, p] = real_b[rows].astype(jnp.bfloat16)
            stage[station, 1, p] = imag_b[rows].astype(jnp.bfloat16)
            for block in range(4):
                at = station * 32 + block * 8
                compact[station] = jnp.where(
                    lane_group == p * 4 + block,
                    jnp.broadcast_to(squares[at : at + 8], (8, 128)),
                    compact[station],
                )
    for station in range(GROUP):
        power_out[station] = compact[station]

    def power_copy(peer):
        return pltpu.make_async_remote_copy(
            src_ref=power_out.at[peer],
            dst_ref=power_in.at[me],
            send_sem=send_power,
            recv_sem=recv_power,
            device_id={"station": peer},
            device_id_type=MESH,
        )

    def beam_copy(peer):
        return pltpu.make_async_remote_copy(
            src_ref=stage.at[peer],
            dst_ref=arrived.at[me],
            send_sem=send_beam,
            recv_sem=recv_beam,
            device_id={"station": peer},
            device_id_type=MESH,
        )

    everyone(lambda peer: power_copy(peer).start())
    for at in BEAM_TURNS:
        beam_copy(others[at]).start()
    power_in[me] = power_out[me]
    own_beam = pltpu.make_async_copy(stage.at[me], arrived.at[me], local_sem.at[8])
    own_beam.start()

    together(power_in, recv_power).wait()
    power = power_in[0]
    for station in range(1, GROUP):
        power = power + power_in[station]
    slot = plane * 2 + core
    power_two[slot] = power
    two_copies = []
    for at, peer in enumerate(seven):
        copy = pltpu.make_async_remote_copy(
            src_ref=power_two.at[slot],
            dst_ref=power_two.at[slot],
            send_sem=send_two.at[at],
            recv_sem=recv_two.at[at],
            device_id=peer,
            device_id_type=MESH,
        )
        copy.start()
        two_copies.append(copy)

    together(first_out, send_first).wait()
    together(field, send_x).wait()
    together(power_out, send_power).wait()
    for copy in image_copies:
        copy.wait_send()
    together(stage, send_beam).wait()
    together(arrived, recv_beam).wait()
    own_beam.wait()

    for copy in two_copies:
        copy.wait_recv()
    power = power_two[0]
    for at in range(1, 8):
        power = power + power_two[at]
    rescale[...] = lax.rsqrt(power / (CHANNELS * TIME) + 1e-06)

    for copy in two_copies:
        copy.wait_send()


def normalise(arrived, rescale, basis, out, sub_hbm, result, sub, sem):
    scales = []
    for p in range(2):
        rows = []
        for block in range(4):
            lane = (p * 4 + block) * 8
            rows.append(jnp.broadcast_to(rescale[:, lane : lane + 1], (8, 128)))
        scales.append(jnp.concatenate(rows, axis=0))
    copies = []
    for c in range(8):
        for side in range(2):
            for part in range(2):
                for p in range(2):
                    value = arrived[2 * c + side, part, p].astype(jnp.float32) * scales[p]
                    result[part, c, p, :, side * 128 : (side + 1) * 128] = value.astype(jnp.bfloat16)
        copy = pltpu.make_async_copy(result.at[:, c], out.at[:, c], sem.at[c])
        copy.start()
        copies.append(copy)
    for c in range(8):
        for p in range(2):
            for part in range(2):
                at = part * 4
                sub[part, c, pl.ds(p, 4, stride=2), :] = basis[2 * c, at : at + 4, 64 + p * 32 : 96 + p * 32]
    copy = pltpu.make_async_copy(sub, sub_hbm, sem.at[8])
    copy.start()
    copies.append(copy)
    for copy in copies:
        copy.wait()


def body(voltages, start_seed, beam_phase, station_delay):
    vmem = pl.BlockSpec(memory_space=pltpu.VMEM)
    hbm = pl.BlockSpec(memory_space=pltpu.MemorySpace.HBM)
    anywhere = pl.BlockSpec(memory_space=pl.ANY)
    dma = pltpu.SemaphoreType.DMA
    f32, bf16 = jnp.float32, jnp.bfloat16
    def kept(value):
        return pltpu.with_memory_space_constraint(value, pltpu.MemorySpace.HBM)

    operands = (
        voltages,
        start_seed.reshape(2, 8, 8, 32),
        beam_phase,
        station_delay.reshape(1, STATIONS),
    )
    arrived, rescale, basis = pl.pallas_call(
        exchange,
        out_shape=(
            jax.ShapeDtypeStruct((16, 2, 2, 32, 128), bf16),
            jax.ShapeDtypeStruct((8, 128), f32),
            jax.ShapeDtypeStruct((GROUP, 8, 128), f32),
        ),
        in_specs=[hbm] * 4,
        out_specs=(vmem, vmem, vmem),
        scratch_shapes=[
            pltpu.VMEM((8, 2, 2, 32, 256), bf16),
            pltpu.VMEM((2, 8, 8, 32), jnp.int32),
            pltpu.VMEM((512, 512), jnp.int32),
            pltpu.VMEM((1, 512), jnp.int32),
            pltpu.VMEM((GROUP, 2, 32, 256), bf16),
            pltpu.VMEM((GROUP, 8, 128), f32),
            pltpu.VMEM((GROUP, 8, 128), f32),
            pltpu.VMEM((ITERS, QUARTERS, 8, 1024), f32),
            pltpu.VMEM((2, 512, 512), bf16),
            pltpu.VMEM((GROUP, 2, 2, 32, 128), bf16),
            pltpu.VMEM((GROUP, 8, 128), f32),
            pltpu.VMEM((8, 8, 128), f32),
            dma((10,)),
            dma(()),
            dma(()),
            dma(()),
            dma(()),
            dma((ITERS, 3)),
            dma((ITERS, 3)),
            dma(()),
            dma(()),
            dma((7,)),
            dma((7,)),
            dma(()),
            dma(()),
        ],
        compiler_params=pltpu.CompilerParams(
            collective_id=0, has_side_effects=True, vmem_limit_bytes=40 * 1024 * 1024
        ),
    )(*map(kept, operands))
    beam_output, subspace = pl.pallas_call(
        normalise,
        out_shape=(
            jax.ShapeDtypeStruct((2, 8, 2, 32, 256), bf16),
            jax.ShapeDtypeStruct((2, 8, 8, 32), f32),
        ),
        in_specs=[vmem] * 3,
        out_specs=(anywhere, anywhere),
        scratch_shapes=[
            pltpu.VMEM((2, 8, 2, 32, 256), bf16),
            pltpu.VMEM((2, 8, 8, 32), f32),
            dma((9,)),
        ],
        compiler_params=pltpu.CompilerParams(vmem_limit_bytes=40 * 1024 * 1024),
    )(arrived, rescale, basis)
    return beam_output, subspace.reshape(2, 8, 4, 2, 32)


def solution(mesh):
    in_specs = (
        P(None, "channel", None, "station", "tm"),
        P(None, "channel", None, None, "station"),
        P(),
        P(),
    )
    out_specs = (
        P(None, "channel", None, "station", "tm"),
        P(None, "channel", None, None, "station"),
    )
    return jax.shard_map(body, mesh=mesh, in_specs=in_specs, out_specs=out_specs, check_vma=False)
```

```python
import functools

import jax
import jax.numpy as jnp
from jax import lax
from jax.experimental import pallas as pl
from jax.experimental.pallas import tpu as pltpu
from jax.sharding import PartitionSpec as P

STATIONS = 512
CHANNELS = 32
ITERS = 3
PHASES = 1024
TIME = 512
RANK = 4
GROUP = 16
QUARTERS = 4

MESH = pl.DeviceIdType.MESH

COS_TERMS = (
    0.9999999998855527,
    -4.934802185863431,
    4.058711817242859,
    -1.3352602861671086,
    0.23532082553812417,
    -0.025785808775470303,
    0.0019043289643584185,
    -8.86909374720357e-05,
)
SIN_TERMS = (
    3.141592653568331,
    -5.167712777297557,
    2.5501639819324518,
    -0.599264064211247,
    0.0821440508162118,
    -0.007366486943808629,
    0.000461586777512204,
    -1.8944663042615234e-05,
)


FARTHEST_FIRST = (
    (2, 2),
    (2, 1),
    (2, 3),
    (1, 2),
    (3, 2),
    (1, 1),
    (3, 3),
    (1, 3),
    (3, 1),
    (2, 0),
    (0, 2),
    (1, 0),
    (3, 0),
    (0, 1),
    (0, 3),
)
BEAM_TURNS = (0, 13, 1, 12, 2, 11, 3, 14, 4, 9, 10, 5, 6, 7, 8)


def horner(terms, scale, v):
    total = jnp.full_like(v, terms[-1] * scale)
    for term in terms[-2::-1]:
        total = total * v + jnp.float32(term * scale)
    return total


def three_parts(value):
    high = value.astype(jnp.bfloat16)
    rest = value - high.astype(jnp.float32)
    middle = rest.astype(jnp.bfloat16)
    low = (rest - middle.astype(jnp.float32)).astype(jnp.bfloat16)
    return high, middle, low


def sum_of_three(rows):
    return rows[0:8] + (rows[8:16] + rows[16:24])


def half_swap(rows):
    return pltpu.roll(rows, 4, 0)


def exchange(
    volt,
    seed_hbm,
    phase,
    delay_hbm,
    arrived,
    rescale,
    power_in,
    local_x,
    seed,
    phases,
    delay,
    field,
    first_out,
    first_in,
    image,
    weights,
    stage,
    power_out,
    power_two,
    local_sem,
    send_x,
    recv_x,
    send_first,
    recv_first,
    send_image,
    recv_image,
    send_power,
    recv_power,
    send_two,
    recv_two,
    send_beam,
    recv_beam,
):
    core = lax.axis_index("tm")
    me = lax.axis_index("station")
    plane = lax.axis_index("channel")
    mine = me // 2
    half = me % 2
    twin = me + 1 - 2 * half
    quarter = core * 2 + half

    others = []
    for across, along in FARTHEST_FIRST:
        row = (me // 4 + across) % 4
        column = (me % 4 + along) % 4
        others.append(row * 4 + column)

    def everyone(start):
        for peer in others:
            start(peer)

    def together(buffer, sem):
        part = buffer.at[pl.ds(0, GROUP - 1)]
        return pltpu.make_async_copy(part, part, sem)

    loads = [
        pltpu.make_async_copy(
            volt.at[part, :, :, :, pl.ds(side * 128, 128)],
            local_x.at[:, side, :, :, pl.ds(part * 128, 128)],
            local_sem.at[part * 2 + side],
        )
        for part in range(2)
        for side in range(2)
    ]
    loads.append(pltpu.make_async_copy(seed_hbm, seed, local_sem.at[4]))
    loads.append(pltpu.make_async_copy(phase, phases, local_sem.at[5]))
    loads.append(pltpu.make_async_copy(delay_hbm, delay, local_sem.at[6]))

    barrier = pltpu.get_barrier_semaphore()
    three = (
        {"tm": 1 - core, "station": twin},
        {"station": twin},
        {"tm": 1 - core},
    )
    seven = [{"channel": (plane + 2) % 4}, {"tm": 1 - core, "channel": (plane + 2) % 4}]
    for step in (1, 3):
        other = (plane + step) % 4
        seven.append({"channel": other})
        seven.append({"tm": 1 - core, "channel": other})
    seven.append({"tm": 1 - core})

    def greet(peer):
        pl.semaphore_signal(barrier, inc=1, device_id=peer, device_id_type=MESH)

    everyone(lambda peer: greet({"station": peer}))
    for peer in seven:
        greet(peer)
    greet(three[0])
    for load in loads:
        load.start()
    row = lax.broadcasted_iota(jnp.int32, (8, 128), 0)
    upper = jnp.where(row < 4, 1.0, -1.0).astype(jnp.float32)

    for load in loads[:5]:
        load.wait()
    for c in range(8):
        left = []
        for p in range(2):
            real_s = seed[0, c, pl.ds(p, 4, stride=2), :].astype(jnp.float32)
            imag_s = seed[1, c, pl.ds(p, 4, stride=2), :].astype(jnp.float32)
            left.append(jnp.concatenate([real_s, imag_s], axis=0))
        left = jnp.concatenate(left, axis=1).astype(jnp.bfloat16)
        for side in range(2):
            right = local_x[c, side].reshape(64, 256)
            rows = jnp.dot(left, right, preferred_element_type=jnp.float32)
            share = half_swap(rows[:, 128:256]) + upper * rows[:, 0:128]
            first_out[2 * c + side] = share.astype(jnp.bfloat16)

    pl.semaphore_wait(barrier, GROUP - 1 + len(seven) + 1)

    def first_copy(peer):
        return pltpu.make_async_remote_copy(
            src_ref=first_out.at[peer],
            dst_ref=first_in.at[me],
            send_sem=send_first,
            recv_sem=recv_first,
            device_id={"station": peer},
            device_id_type=MESH,
        )

    def x_copy(peer):
        return pltpu.make_async_remote_copy(
            src_ref=local_x.at[peer // 2, peer % 2],
            dst_ref=field.at[me],
            send_sem=send_x,
            recv_sem=recv_x,
            device_id={"station": peer},
            device_id_type=MESH,
        )

    for peer in others[:3]:
        x_copy(peer).start()
    everyone(lambda peer: first_copy(peer).start())
    for peer in others[3:]:
        x_copy(peer).start()
    own_x = pltpu.make_async_copy(local_x.at[mine, half], field.at[me], local_sem.at[7])
    own_x.start()
    first_in[me] = first_out[me]

    loads[5].wait()
    loads[6].wait()
    number = plane * 8 + mine + 1
    norming = STATIONS**-0.5

    def weight_rows(block, carry):
        rows = pl.ds(pl.multiple_of(block * 32, 32), 32)
        index = (phases[rows, :] + delay[...]) * number
        wrapped = (index + PHASES // 2) & (PHASES - 1)
        u = (wrapped - PHASES // 2).astype(jnp.float32) * jnp.float32(2.0 / PHASES)
        v = u * u
        weights[0, rows, :] = horner(COS_TERMS, norming, v).astype(jnp.bfloat16)
        weights[1, rows, :] = (u * horner(SIN_TERMS, -norming, v)).astype(jnp.bfloat16)
        return carry

    lax.fori_loop(0, 16, weight_rows, 0)

    together(first_in, recv_first).wait()
    together(field, recv_x).wait()
    own_x.wait()

    def turned(c8):
        return jnp.concatenate([c8, half_swap(c8) * upper], axis=1)

    def apply_field(c8):
        left = jnp.concatenate(three_parts(turned(c8)), axis=0)
        right = field[...].reshape(1024, 256)
        rows = lax.dot_general(left, right, (((1,), (1,)), ((), ())), preferred_element_type=jnp.float32)
        return sum_of_three(rows)

    def coefficients(h8):
        left = jnp.concatenate(three_parts(h8), axis=0)
        rows = jnp.dot(left, field[...].reshape(1024, 256), preferred_element_type=jnp.float32)
        rows = sum_of_three(rows)
        return rows[:, 0:128] - upper * half_swap(rows[:, 128:256])

    def factor(h8):
        shifted = []
        for shift in range(4):
            moved = h8 * (pltpu.roll(h8, shift, 0) if shift else h8)
            lanes = moved[:, 0:128]
            for block in range(1, 8):
                lanes = lanes + moved[:, block * 128 : (block + 1) * 128]
            dots = jnp.broadcast_to(jnp.sum(lanes, axis=1, keepdims=True), (8, 128))
            swapped = half_swap(dots)
            shifted.append((dots + swapped, dots - swapped))

        def pick(rows, at):
            return jnp.broadcast_to(rows[at : at + 1, :], (8, 128))

        low = {}
        inverse = {}
        for column in range(RANK):
            diagonal = pick(shifted[0][0], column)
            for middle in range(column):
                re, im = low[column, middle]
                diagonal = diagonal - (re * re + im * im)
            inverse[column] = lax.rsqrt(diagonal)
            for at in range(column + 1, RANK):
                distance = at - column
                re = pick(shifted[distance][0], at)
                im = pick(shifted[4 - distance][1], column)
                for middle in range(column):
                    a_re, a_im = low[at, middle]
                    b_re, b_im = low[column, middle]
                    re = re - (a_re * b_re + a_im * b_im)
                    im = im - (a_im * b_re - a_re * b_im)
                low[at, column] = (re * inverse[column], im * inverse[column])
        return low, inverse

    def solve(low, inverse, rows):
        width = rows.shape[1]
        repeat = width // 128

        def wide(value):
            return value if repeat == 1 else jnp.concatenate([value] * repeat, axis=1)

        done = []
        for at in range(RANK):
            re = jnp.broadcast_to(rows[at : at + 1, :], (8, width))
            im = jnp.broadcast_to(rows[at + 4 : at + 5, :], (8, width))
            for middle in range(at):
                l_re, l_im = low[at, middle]
                l_re, l_im = wide(l_re), wide(l_im)
                d_re, d_im = done[middle]
                re = re - (l_re * d_re - l_im * d_im)
                im = im - (l_re * d_im + l_im * d_re)
            scale = wide(inverse[at])
            done.append((re * scale, im * scale))
        at_row = lax.broadcasted_iota(jnp.int32, (8, width), 0)
        total = done[3][1]
        for at in range(RANK):
            total = jnp.where(at_row == at, done[at][0], total)
            if at < 3:
                total = jnp.where(at_row == at + 4, done[at][1], total)
        return total

    coefficient = jnp.sum(first_in[...].astype(jnp.float32), axis=0)

    image_copies = []
    for iteration in range(ITERS):
        image[iteration, quarter] = apply_field(coefficient)
        for at, peer in enumerate(three):
            copy = pltpu.make_async_remote_copy(
                src_ref=image.at[iteration, quarter],
                dst_ref=image.at[iteration, quarter],
                send_sem=send_image.at[iteration, at],
                recv_sem=recv_image.at[iteration, at],
                device_id=peer,
                device_id_type=MESH,
            )
            copy.start()
            image_copies.append(copy)
        for copy in image_copies[-3:]:
            copy.wait_recv()
        summed = (image[iteration, 0] + image[iteration, 1]) + (image[iteration, 2] + image[iteration, 3])
        raw = coefficients(summed)
        low, inverse = factor(summed)
        coefficient = solve(low, inverse, raw)
    basis = solve(low, inverse, summed)

    def six(parts, which):
        return jnp.concatenate([parts[at] for at in which], axis=0)

    left = six(three_parts(basis), (0, 0, 1, 0, 1, 2))
    right = six(three_parts(turned(coefficient)), (0, 1, 0, 2, 1, 0))
    removed = lax.dot_general(left, right, (((0,), (0,)), ((), ())), preferred_element_type=jnp.float32)
    cleaned = field[...].reshape(1024, 256).astype(jnp.float32) - removed
    cleaned = cleaned.astype(jnp.bfloat16).reshape(GROUP, 2, 32, 256)
    lane_group = lax.broadcasted_iota(jnp.int32, (8, 128), 1) // 8
    compact = []
    for block in range(8):
        lanes = basis[:, block * 128 : (block + 1) * 128] * upper
        compact += [pltpu.roll(lanes, 64, 1), lanes]
    for p in range(2):
        ours = cleaned[:, p].reshape(512, 256)
        on_real = jnp.dot(weights[0], ours, preferred_element_type=jnp.float32)
        on_imag = jnp.dot(weights[1], ours, preferred_element_type=jnp.float32)
        real_b = on_real[:, 0:128] - on_imag[:, 128:256]
        imag_b = on_real[:, 128:256] + on_imag[:, 0:128]
        squares = jnp.sum(real_b * real_b + imag_b * imag_b, axis=1, keepdims=True)
        for station in range(GROUP):
            rows = slice(station * 32, (station + 1) * 32)
            stage[station, 0, p] = real_b[rows].astype(jnp.bfloat16)
            stage[station, 1, p] = imag_b[rows].astype(jnp.bfloat16)
            for block in range(4):
                at = station * 32 + block * 8
                compact[station] = jnp.where(
                    lane_group == p * 4 + block,
                    jnp.broadcast_to(squares[at : at + 8], (8, 128)),
                    compact[station],
                )
    for station in range(GROUP):
        power_out[station] = compact[station]

    def power_copy(peer):
        return pltpu.make_async_remote_copy(
            src_ref=power_out.at[peer],
            dst_ref=power_in.at[me],
            send_sem=send_power,
            recv_sem=recv_power,
            device_id={"station": peer},
            device_id_type=MESH,
        )

    def beam_copy(peer):
        return pltpu.make_async_remote_copy(
            src_ref=stage.at[peer],
            dst_ref=arrived.at[me],
            send_sem=send_beam,
            recv_sem=recv_beam,
            device_id={"station": peer},
            device_id_type=MESH,
        )

    everyone(lambda peer: power_copy(peer).start())
    for at in BEAM_TURNS:
        beam_copy(others[at]).start()
    power_in[me] = power_out[me]
    own_beam = pltpu.make_async_copy(stage.at[me], arrived.at[me], local_sem.at[8])
    own_beam.start()

    together(power_in, recv_power).wait()
    power = power_in[0]
    for station in range(1, GROUP):
        power = power + power_in[station]
    slot = plane * 2 + core
    power_two[slot] = power
    two_copies = []
    for at, peer in enumerate(seven):
        copy = pltpu.make_async_remote_copy(
            src_ref=power_two.at[slot],
            dst_ref=power_two.at[slot],
            send_sem=send_two.at[at],
            recv_sem=recv_two.at[at],
            device_id=peer,
            device_id_type=MESH,
        )
        copy.start()
        two_copies.append(copy)

    together(first_out, send_first).wait()
    together(field, send_x).wait()
    together(power_out, send_power).wait()
    for copy in image_copies:
        copy.wait_send()
    together(stage, send_beam).wait()
    together(arrived, recv_beam).wait()
    own_beam.wait()

    for copy in two_copies:
        copy.wait_recv()
    power = power_two[0]
    for at in range(1, 8):
        power = power + power_two[at]
    rescale[...] = lax.rsqrt(power / (CHANNELS * TIME) + 1e-06)

    for copy in two_copies:
        copy.wait_send()


def normalise(arrived, rescale, basis, out, sub_hbm, result, sub, sem):
    scales = []
    for p in range(2):
        rows = []
        for block in range(4):
            lane = (p * 4 + block) * 8
            rows.append(jnp.broadcast_to(rescale[:, lane : lane + 1], (8, 128)))
        scales.append(jnp.concatenate(rows, axis=0))
    copies = []
    for c in range(8):
        for side in range(2):
            for part in range(2):
                for p in range(2):
                    value = arrived[2 * c + side, part, p].astype(jnp.float32) * scales[p]
                    result[part, c, p, :, side * 128 : (side + 1) * 128] = value.astype(jnp.bfloat16)
        copy = pltpu.make_async_copy(result.at[:, c], out.at[:, c], sem.at[c])
        copy.start()
        copies.append(copy)
    for c in range(8):
        for p in range(2):
            for part in range(2):
                at = part * 4
                sub[part, c, pl.ds(p, 4, stride=2), :] = basis[2 * c, at : at + 4, 64 + p * 32 : 96 + p * 32]
    copy = pltpu.make_async_copy(sub, sub_hbm, sem.at[8])
    copy.start()
    copies.append(copy)
    for copy in copies:
        copy.wait()


def body(voltages, start_seed, beam_phase, station_delay):
    vmem = pl.BlockSpec(memory_space=pltpu.VMEM)
    hbm = pl.BlockSpec(memory_space=pltpu.MemorySpace.HBM)
    anywhere = pl.BlockSpec(memory_space=pl.ANY)
    dma = pltpu.SemaphoreType.DMA
    f32, bf16 = jnp.float32, jnp.bfloat16
    def kept(value):
        return pltpu.with_memory_space_constraint(value, pltpu.MemorySpace.HBM)

    operands = (
        voltages,
        start_seed.reshape(2, 8, 8, 32),
        beam_phase,
        station_delay.reshape(1, STATIONS),
    )
    arrived, rescale, basis = pl.pallas_call(
        exchange,
        out_shape=(
            jax.ShapeDtypeStruct((16, 2, 2, 32, 128), bf16),
            jax.ShapeDtypeStruct((8, 128), f32),
            jax.ShapeDtypeStruct((GROUP, 8, 128), f32),
        ),
        in_specs=[hbm] * 4,
        out_specs=(vmem, vmem, vmem),
        scratch_shapes=[
            pltpu.VMEM((8, 2, 2, 32, 256), bf16),
            pltpu.VMEM((2, 8, 8, 32), jnp.int32),
            pltpu.VMEM((512, 512), jnp.int32),
            pltpu.VMEM((1, 512), jnp.int32),
            pltpu.VMEM((GROUP, 2, 32, 256), bf16),
            pltpu.VMEM((GROUP, 8, 128), bf16),
            pltpu.VMEM((GROUP, 8, 128), bf16),
            pltpu.VMEM((ITERS, QUARTERS, 8, 1024), f32),
            pltpu.VMEM((2, 512, 512), bf16),
            pltpu.VMEM((GROUP, 2, 2, 32, 128), bf16),
            pltpu.VMEM((GROUP, 8, 128), f32),
            pltpu.VMEM((8, 8, 128), f32),
            dma((10,)),
            dma(()),
            dma(()),
            dma(()),
            dma(()),
            dma((ITERS, 3)),
            dma((ITERS, 3)),
            dma(()),
            dma(()),
            dma((7,)),
            dma((7,)),
            dma(()),
            dma(()),
        ],
        compiler_params=pltpu.CompilerParams(
            collective_id=0, has_side_effects=True, vmem_limit_bytes=40 * 1024 * 1024
        ),
    )(*map(kept, operands))
    beam_output, subspace = pl.pallas_call(
        normalise,
        out_shape=(
            jax.ShapeDtypeStruct((2, 8, 2, 32, 256), bf16),
            jax.ShapeDtypeStruct((2, 8, 8, 32), f32),
        ),
        in_specs=[vmem] * 3,
        out_specs=(anywhere, anywhere),
        scratch_shapes=[
            pltpu.VMEM((2, 8, 2, 32, 256), bf16),
            pltpu.VMEM((2, 8, 8, 32), f32),
            dma((9,)),
        ],
        compiler_params=pltpu.CompilerParams(vmem_limit_bytes=40 * 1024 * 1024),
    )(arrived, rescale, basis)
    return beam_output, subspace.reshape(2, 8, 4, 2, 32)


def solution(mesh):
    in_specs = (
        P(None, "channel", None, "station", "tm"),
        P(None, "channel", None, None, "station"),
        P(),
        P(),
    )
    out_specs = (
        P(None, "channel", None, "station", "tm"),
        P(None, "channel", None, None, "station"),
    )
    return jax.shard_map(body, mesh=mesh, in_specs=in_specs, out_specs=out_specs, check_vma=False)
```

```python
import functools

import jax
import jax.numpy as jnp
from jax import lax
from jax.experimental import pallas as pl
from jax.experimental.pallas import tpu as pltpu
from jax.sharding import PartitionSpec as P

STATIONS = 512
CHANNELS = 32
ITERS = 3
PHASES = 1024
TIME = 512
RANK = 4
GROUP = 16
QUARTERS = 4

MESH = pl.DeviceIdType.MESH

COS_TERMS = (
    0.9999999998855527,
    -4.934802185863431,
    4.058711817242859,
    -1.3352602861671086,
    0.23532082553812417,
    -0.025785808775470303,
    0.0019043289643584185,
    -8.86909374720357e-05,
)
SIN_TERMS = (
    3.141592653568331,
    -5.167712777297557,
    2.5501639819324518,
    -0.599264064211247,
    0.0821440508162118,
    -0.007366486943808629,
    0.000461586777512204,
    -1.8944663042615234e-05,
)


FARTHEST_FIRST = (
    (2, 2),
    (2, 1),
    (2, 3),
    (1, 2),
    (3, 2),
    (1, 1),
    (3, 3),
    (1, 3),
    (3, 1),
    (2, 0),
    (0, 2),
    (1, 0),
    (3, 0),
    (0, 1),
    (0, 3),
)
BEAM_TURNS = (0, 13, 1, 12, 2, 11, 3, 14, 4, 9, 10, 5, 6, 7, 8)


def horner(terms, scale, v):
    total = jnp.full_like(v, terms[-1] * scale)
    for term in terms[-2::-1]:
        total = total * v + jnp.float32(term * scale)
    return total


def three_parts(value):
    high = value.astype(jnp.bfloat16)
    rest = value - high.astype(jnp.float32)
    middle = rest.astype(jnp.bfloat16)
    low = (rest - middle.astype(jnp.float32)).astype(jnp.bfloat16)
    return high, middle, low


def sum_of_three(rows):
    return rows[0:8] + (rows[8:16] + rows[16:24])


def half_swap(rows):
    return pltpu.roll(rows, 4, 0)


def exchange(
    volt,
    seed_hbm,
    phase,
    delay_hbm,
    arrived,
    rescale,
    sub,
    local_x,
    seed,
    phases,
    delay,
    field,
    first_out,
    first_in,
    image,
    weights,
    stage,
    power_out,
    power_in,
    power_two,
    local_sem,
    send_x,
    recv_x,
    send_first,
    recv_first,
    send_image,
    recv_image,
    send_power,
    recv_power,
    send_two,
    recv_two,
    send_beam,
    recv_beam,
):
    core = lax.axis_index("tm")
    me = lax.axis_index("station")
    plane = lax.axis_index("channel")
    mine = me // 2
    half = me % 2
    twin = me + 1 - 2 * half
    quarter = core * 2 + half

    others = []
    for across, along in FARTHEST_FIRST:
        row = (me // 4 + across) % 4
        column = (me % 4 + along) % 4
        others.append(row * 4 + column)

    def everyone(start):
        for peer in others:
            start(peer)

    def together(buffer, sem):
        part = buffer.at[pl.ds(0, GROUP - 1)]
        return pltpu.make_async_copy(part, part, sem)

    loads = [
        pltpu.make_async_copy(
            volt.at[part, :, :, :, pl.ds(side * 128, 128)],
            local_x.at[:, side, :, :, pl.ds(part * 128, 128)],
            local_sem.at[part * 2 + side],
        )
        for part in range(2)
        for side in range(2)
    ]
    loads.append(pltpu.make_async_copy(seed_hbm, seed, local_sem.at[4]))
    loads.append(pltpu.make_async_copy(phase, phases, local_sem.at[5]))
    loads.append(pltpu.make_async_copy(delay_hbm, delay, local_sem.at[6]))

    barrier = pltpu.get_barrier_semaphore()
    three = (
        {"tm": 1 - core, "station": twin},
        {"station": twin},
        {"tm": 1 - core},
    )
    seven = [{"channel": (plane + 2) % 4}, {"tm": 1 - core, "channel": (plane + 2) % 4}]
    for step in (1, 3):
        other = (plane + step) % 4
        seven.append({"channel": other})
        seven.append({"tm": 1 - core, "channel": other})
    seven.append({"tm": 1 - core})

    def greet(peer):
        pl.semaphore_signal(barrier, inc=1, device_id=peer, device_id_type=MESH)

    everyone(lambda peer: greet({"station": peer}))
    for peer in seven:
        greet(peer)
    greet(three[0])
    for load in loads:
        load.start()
    row = lax.broadcasted_iota(jnp.int32, (8, 128), 0)
    upper = jnp.where(row < 4, 1.0, -1.0).astype(jnp.float32)

    for load in loads[:5]:
        load.wait()
    for c in range(8):
        left = []
        for p in range(2):
            real_s = seed[0, c, pl.ds(p, 4, stride=2), :].astype(jnp.float32)
            imag_s = seed[1, c, pl.ds(p, 4, stride=2), :].astype(jnp.float32)
            left.append(jnp.concatenate([real_s, imag_s], axis=0))
        left = jnp.concatenate(left, axis=1).astype(jnp.bfloat16)
        for side in range(2):
            right = local_x[c, side].reshape(64, 256)
            rows = jnp.dot(left, right, preferred_element_type=jnp.float32)
            share = half_swap(rows[:, 128:256]) + upper * rows[:, 0:128]
            first_out[2 * c + side] = share.astype(jnp.bfloat16)

    pl.semaphore_wait(barrier, GROUP - 1 + len(seven) + 1)

    def first_copy(peer):
        return pltpu.make_async_remote_copy(
            src_ref=first_out.at[peer],
            dst_ref=first_in.at[me],
            send_sem=send_first,
            recv_sem=recv_first,
            device_id={"station": peer},
            device_id_type=MESH,
        )

    def x_copy(peer):
        return pltpu.make_async_remote_copy(
            src_ref=local_x.at[peer // 2, peer % 2],
            dst_ref=field.at[me],
            send_sem=send_x,
            recv_sem=recv_x,
            device_id={"station": peer},
            device_id_type=MESH,
        )

    for peer in others[:3]:
        x_copy(peer).start()
    everyone(lambda peer: first_copy(peer).start())
    for peer in others[3:]:
        x_copy(peer).start()
    own_x = pltpu.make_async_copy(local_x.at[mine, half], field.at[me], local_sem.at[7])
    own_x.start()
    first_in[me] = first_out[me]

    loads[5].wait()
    loads[6].wait()
    number = plane * 8 + mine + 1
    norming = STATIONS**-0.5

    def weight_rows(block, carry):
        rows = pl.ds(pl.multiple_of(block * 32, 32), 32)
        index = (phases[rows, :] + delay[...]) * number
        wrapped = (index + PHASES // 2) & (PHASES - 1)
        u = (wrapped - PHASES // 2).astype(jnp.float32) * jnp.float32(2.0 / PHASES)
        v = u * u
        weights[0, rows, :] = horner(COS_TERMS, norming, v).astype(jnp.bfloat16)
        weights[1, rows, :] = (u * horner(SIN_TERMS, -norming, v)).astype(jnp.bfloat16)
        return carry

    lax.fori_loop(0, 16, weight_rows, 0)

    together(first_in, recv_first).wait()
    together(field, recv_x).wait()
    own_x.wait()

    def turned(c8):
        return jnp.concatenate([c8, half_swap(c8) * upper], axis=1)

    def apply_field(c8):
        left = jnp.concatenate(three_parts(turned(c8)), axis=0)
        right = field[...].reshape(1024, 256)
        rows = lax.dot_general(left, right, (((1,), (1,)), ((), ())), preferred_element_type=jnp.float32)
        return sum_of_three(rows)

    def coefficients(h8):
        left = jnp.concatenate(three_parts(h8), axis=0)
        rows = jnp.dot(left, field[...].reshape(1024, 256), preferred_element_type=jnp.float32)
        rows = sum_of_three(rows)
        return rows[:, 0:128] - upper * half_swap(rows[:, 128:256])

    def factor(h8):
        shifted = []
        for shift in range(4):
            moved = h8 * (pltpu.roll(h8, shift, 0) if shift else h8)
            lanes = moved[:, 0:128]
            for block in range(1, 8):
                lanes = lanes + moved[:, block * 128 : (block + 1) * 128]
            dots = jnp.broadcast_to(jnp.sum(lanes, axis=1, keepdims=True), (8, 128))
            swapped = half_swap(dots)
            shifted.append((dots + swapped, dots - swapped))

        def pick(rows, at):
            return jnp.broadcast_to(rows[at : at + 1, :], (8, 128))

        low = {}
        inverse = {}
        for column in range(RANK):
            diagonal = pick(shifted[0][0], column)
            for middle in range(column):
                re, im = low[column, middle]
                diagonal = diagonal - (re * re + im * im)
            inverse[column] = lax.rsqrt(diagonal)
            for at in range(column + 1, RANK):
                distance = at - column
                re = pick(shifted[distance][0], at)
                im = pick(shifted[4 - distance][1], column)
                for middle in range(column):
                    a_re, a_im = low[at, middle]
                    b_re, b_im = low[column, middle]
                    re = re - (a_re * b_re + a_im * b_im)
                    im = im - (a_im * b_re - a_re * b_im)
                low[at, column] = (re * inverse[column], im * inverse[column])
        return low, inverse

    def solve(low, inverse, rows):
        width = rows.shape[1]
        repeat = width // 128

        def wide(value):
            return value if repeat == 1 else jnp.concatenate([value] * repeat, axis=1)

        done = []
        for at in range(RANK):
            re = jnp.broadcast_to(rows[at : at + 1, :], (8, width))
            im = jnp.broadcast_to(rows[at + 4 : at + 5, :], (8, width))
            for middle in range(at):
                l_re, l_im = low[at, middle]
                l_re, l_im = wide(l_re), wide(l_im)
                d_re, d_im = done[middle]
                re = re - (l_re * d_re - l_im * d_im)
                im = im - (l_re * d_im + l_im * d_re)
            scale = wide(inverse[at])
            done.append((re * scale, im * scale))
        at_row = lax.broadcasted_iota(jnp.int32, (8, width), 0)
        total = done[3][1]
        for at in range(RANK):
            total = jnp.where(at_row == at, done[at][0], total)
            if at < 3:
                total = jnp.where(at_row == at + 4, done[at][1], total)
        return total

    coefficient = jnp.sum(first_in[...].astype(jnp.float32), axis=0)

    image_copies = []
    for iteration in range(ITERS):
        image[iteration, quarter] = apply_field(coefficient)
        for at, peer in enumerate(three):
            copy = pltpu.make_async_remote_copy(
                src_ref=image.at[iteration, quarter],
                dst_ref=image.at[iteration, quarter],
                send_sem=send_image.at[iteration, at],
                recv_sem=recv_image.at[iteration, at],
                device_id=peer,
                device_id_type=MESH,
            )
            copy.start()
            image_copies.append(copy)
        for copy in image_copies[-3:]:
            copy.wait_recv()
        summed = (image[iteration, 0] + image[iteration, 1]) + (image[iteration, 2] + image[iteration, 3])
        raw = coefficients(summed)
        low, inverse = factor(summed)
        coefficient = solve(low, inverse, raw)
    basis = solve(low, inverse, summed)

    def six(parts, which):
        return jnp.concatenate([parts[at] for at in which], axis=0)

    left = six(three_parts(basis), (0, 0, 1, 0, 1, 2))
    right = six(three_parts(turned(coefficient)), (0, 1, 0, 2, 1, 0))
    removed = lax.dot_general(left, right, (((0,), (0,)), ((), ())), preferred_element_type=jnp.float32)
    cleaned = field[...].reshape(1024, 256).astype(jnp.float32) - removed
    cleaned = cleaned.astype(jnp.bfloat16).reshape(GROUP, 2, 32, 256)
    lane_group = lax.broadcasted_iota(jnp.int32, (8, 128), 1) // 8
    compact = []
    for block in range(8):
        lanes = basis[:, block * 128 : (block + 1) * 128] * upper
        compact += [pltpu.roll(lanes, 64, 1), lanes]
    for p in range(2):
        ours = cleaned[:, p].reshape(512, 256)
        on_real = jnp.dot(weights[0], ours, preferred_element_type=jnp.float32)
        on_imag = jnp.dot(weights[1], ours, preferred_element_type=jnp.float32)
        real_b = on_real[:, 0:128] - on_imag[:, 128:256]
        imag_b = on_real[:, 128:256] + on_imag[:, 0:128]
        squares = jnp.sum(real_b * real_b + imag_b * imag_b, axis=1, keepdims=True)
        for station in range(GROUP):
            rows = slice(station * 32, (station + 1) * 32)
            stage[station, 0, p] = real_b[rows].astype(jnp.bfloat16)
            stage[station, 1, p] = imag_b[rows].astype(jnp.bfloat16)
            for block in range(4):
                at = station * 32 + block * 8
                compact[station] = jnp.where(
                    lane_group == p * 4 + block,
                    jnp.broadcast_to(squares[at : at + 8], (8, 128)),
                    compact[station],
                )
    for station in range(GROUP):
        power_out[station] = compact[station]

    def power_copy(peer):
        return pltpu.make_async_remote_copy(
            src_ref=power_out.at[peer],
            dst_ref=power_in.at[me],
            send_sem=send_power,
            recv_sem=recv_power,
            device_id={"station": peer},
            device_id_type=MESH,
        )

    def beam_copy(peer):
        return pltpu.make_async_remote_copy(
            src_ref=stage.at[peer],
            dst_ref=arrived.at[me],
            send_sem=send_beam,
            recv_sem=recv_beam,
            device_id={"station": peer},
            device_id_type=MESH,
        )

    everyone(lambda peer: power_copy(peer).start())
    for at in BEAM_TURNS:
        beam_copy(others[at]).start()
    power_in[me] = power_out[me]
    own_beam = pltpu.make_async_copy(stage.at[me], arrived.at[me], local_sem.at[8])
    own_beam.start()

    together(power_in, recv_power).wait()
    power = power_in[0]
    for station in range(1, GROUP):
        power = power + power_in[station]
    slot = plane * 2 + core
    power_two[slot] = power
    two_copies = []
    for at, peer in enumerate(seven):
        copy = pltpu.make_async_remote_copy(
            src_ref=power_two.at[slot],
            dst_ref=power_two.at[slot],
            send_sem=send_two.at[at],
            recv_sem=recv_two.at[at],
            device_id=peer,
            device_id_type=MESH,
        )
        copy.start()
        two_copies.append(copy)

    for c in range(8):
        for p in range(2):
            for part in range(2):
                at = part * 4
                sub[part, c, pl.ds(p, 4, stride=2), :] = power_in[2 * c, at : at + 4, 64 + p * 32 : 96 + p * 32]

    together(first_out, send_first).wait()
    together(field, send_x).wait()
    together(power_out, send_power).wait()
    for copy in image_copies:
        copy.wait_send()
    together(stage, send_beam).wait()
    together(arrived, recv_beam).wait()
    own_beam.wait()

    for copy in two_copies:
        copy.wait_recv()
    power = power_two[0]
    for at in range(1, 8):
        power = power + power_two[at]
    rescale[...] = lax.rsqrt(power / (CHANNELS * TIME) + 1e-06)

    for copy in two_copies:
        copy.wait_send()


def normalise(arrived, rescale, sub, out, sub_hbm, result, sem):
    copy = pltpu.make_async_copy(sub, sub_hbm, sem.at[8])
    copy.start()
    copies = [copy]
    scales = []
    for p in range(2):
        rows = []
        for block in range(4):
            lane = (p * 4 + block) * 8
            rows.append(jnp.broadcast_to(rescale[:, lane : lane + 1], (8, 128)))
        scales.append(jnp.concatenate(rows, axis=0))
    for c in range(8):
        for side in range(2):
            for part in range(2):
                for p in range(2):
                    value = arrived[2 * c + side, part, p].astype(jnp.float32) * scales[p]
                    result[part, c, p, :, side * 128 : (side + 1) * 128] = value.astype(jnp.bfloat16)
        copy = pltpu.make_async_copy(result.at[:, c], out.at[:, c], sem.at[c])
        copy.start()
        copies.append(copy)
    for copy in copies:
        copy.wait()


def body(voltages, start_seed, beam_phase, station_delay):
    vmem = pl.BlockSpec(memory_space=pltpu.VMEM)
    hbm = pl.BlockSpec(memory_space=pltpu.MemorySpace.HBM)
    anywhere = pl.BlockSpec(memory_space=pl.ANY)
    dma = pltpu.SemaphoreType.DMA
    f32, bf16 = jnp.float32, jnp.bfloat16
    def kept(value):
        return pltpu.with_memory_space_constraint(value, pltpu.MemorySpace.HBM)

    operands = (
        voltages,
        start_seed.reshape(2, 8, 8, 32),
        beam_phase,
        station_delay.reshape(1, STATIONS),
    )
    arrived, rescale, sub = pl.pallas_call(
        exchange,
        out_shape=(
            jax.ShapeDtypeStruct((16, 2, 2, 32, 128), bf16),
            jax.ShapeDtypeStruct((8, 128), f32),
            jax.ShapeDtypeStruct((2, 8, 8, 32), f32),
        ),
        in_specs=[hbm] * 4,
        out_specs=(vmem, vmem, vmem),
        scratch_shapes=[
            pltpu.VMEM((8, 2, 2, 32, 256), bf16),
            pltpu.VMEM((2, 8, 8, 32), jnp.int32),
            pltpu.VMEM((512, 512), jnp.int32),
            pltpu.VMEM((1, 512), jnp.int32),
            pltpu.VMEM((GROUP, 2, 32, 256), bf16),
            pltpu.VMEM((GROUP, 8, 128), bf16),
            pltpu.VMEM((GROUP, 8, 128), bf16),
            pltpu.VMEM((ITERS, QUARTERS, 8, 1024), f32),
            pltpu.VMEM((2, 512, 512), bf16),
            pltpu.VMEM((GROUP, 2, 2, 32, 128), bf16),
            pltpu.VMEM((GROUP, 8, 128), f32),
            pltpu.VMEM((GROUP, 8, 128), f32),
            pltpu.VMEM((8, 8, 128), f32),
            dma((10,)),
            dma(()),
            dma(()),
            dma(()),
            dma(()),
            dma((ITERS, 3)),
            dma((ITERS, 3)),
            dma(()),
            dma(()),
            dma((7,)),
            dma((7,)),
            dma(()),
            dma(()),
        ],
        compiler_params=pltpu.CompilerParams(
            collective_id=0, has_side_effects=True, vmem_limit_bytes=40 * 1024 * 1024
        ),
    )(*map(kept, operands))
    beam_output, subspace = pl.pallas_call(
        normalise,
        out_shape=(
            jax.ShapeDtypeStruct((2, 8, 2, 32, 256), bf16),
            jax.ShapeDtypeStruct((2, 8, 8, 32), f32),
        ),
        in_specs=[vmem] * 3,
        out_specs=(anywhere, anywhere),
        scratch_shapes=[
            pltpu.VMEM((2, 8, 2, 32, 256), bf16),
            dma((9,)),
        ],
        compiler_params=pltpu.CompilerParams(vmem_limit_bytes=40 * 1024 * 1024),
    )(arrived, rescale, sub)
    return beam_output, subspace.reshape(2, 8, 4, 2, 32)


def solution(mesh):
    in_specs = (
        P(None, "channel", None, "station", "tm"),
        P(None, "channel", None, None, "station"),
        P(),
        P(),
    )
    out_specs = (
        P(None, "channel", None, "station", "tm"),
        P(None, "channel", None, None, "station"),
    )
    return jax.shard_map(body, mesh=mesh, in_specs=in_specs, out_specs=out_specs, check_vma=False)
```

```python
import functools

import jax
import jax.numpy as jnp
from jax import lax
from jax.experimental import pallas as pl
from jax.experimental.pallas import tpu as pltpu
from jax.sharding import PartitionSpec as P

STATIONS = 512
CHANNELS = 32
ITERS = 3
PHASES = 1024
TIME = 512
RANK = 4
GROUP = 16
QUARTERS = 4

MESH = pl.DeviceIdType.MESH

COS_TERMS = (
    0.9999999998855527,
    -4.934802185863431,
    4.058711817242859,
    -1.3352602861671086,
    0.23532082553812417,
    -0.025785808775470303,
    0.0019043289643584185,
    -8.86909374720357e-05,
)
SIN_TERMS = (
    3.141592653568331,
    -5.167712777297557,
    2.5501639819324518,
    -0.599264064211247,
    0.0821440508162118,
    -0.007366486943808629,
    0.000461586777512204,
    -1.8944663042615234e-05,
)


FARTHEST_FIRST = (
    (2, 2),
    (2, 1),
    (2, 3),
    (1, 2),
    (3, 2),
    (1, 1),
    (3, 3),
    (1, 3),
    (3, 1),
    (2, 0),
    (0, 2),
    (1, 0),
    (3, 0),
    (0, 1),
    (0, 3),
)
BEAM_TURNS = (0, 13, 1, 12, 2, 11, 3, 14, 4, 9, 10, 5, 6, 7, 8)


def horner(terms, scale, v):
    total = jnp.full_like(v, terms[-1] * scale)
    for term in terms[-2::-1]:
        total = total * v + jnp.float32(term * scale)
    return total


def three_parts(value):
    high = value.astype(jnp.bfloat16)
    rest = value - high.astype(jnp.float32)
    middle = rest.astype(jnp.bfloat16)
    low = (rest - middle.astype(jnp.float32)).astype(jnp.bfloat16)
    return high, middle, low


def sum_of_three(rows):
    return rows[0:8] + (rows[8:16] + rows[16:24])


def half_swap(rows):
    return pltpu.roll(rows, 4, 0)


def exchange(
    volt,
    seed_hbm,
    phase,
    delay_hbm,
    arrived,
    rescale,
    power_in,
    local_x,
    seed,
    phases,
    delay,
    field,
    first_out,
    first_in,
    image,
    weights,
    stage,
    power_out,
    power_two,
    local_sem,
    send_x,
    recv_x,
    send_first,
    recv_first,
    send_image,
    recv_image,
    send_power,
    recv_power,
    send_two,
    recv_two,
    send_beam,
    recv_beam,
):
    core = lax.axis_index("tm")
    me = lax.axis_index("station")
    plane = lax.axis_index("channel")
    mine = me // 2
    half = me % 2
    twin = me + 1 - 2 * half
    quarter = core * 2 + half

    others = []
    for across, along in FARTHEST_FIRST:
        row = (me // 4 + across) % 4
        column = (me % 4 + along) % 4
        others.append(row * 4 + column)

    def everyone(start):
        for peer in others:
            start(peer)

    def together(buffer, sem):
        part = buffer.at[pl.ds(0, GROUP - 1)]
        return pltpu.make_async_copy(part, part, sem)

    loads = [
        pltpu.make_async_copy(
            volt.at[part, :, :, :, pl.ds(side * 128, 128)],
            local_x.at[:, side, :, :, pl.ds(part * 128, 128)],
            local_sem.at[part * 2 + side],
        )
        for part in range(2)
        for side in range(2)
    ]
    loads.append(pltpu.make_async_copy(seed_hbm, seed, local_sem.at[4]))
    loads.append(pltpu.make_async_copy(phase, phases, local_sem.at[5]))
    loads.append(pltpu.make_async_copy(delay_hbm, delay, local_sem.at[6]))

    barrier = pltpu.get_barrier_semaphore()
    three = (
        {"tm": 1 - core, "station": twin},
        {"station": twin},
        {"tm": 1 - core},
    )
    seven = [{"channel": (plane + 2) % 4}, {"tm": 1 - core, "channel": (plane + 2) % 4}]
    for step in (1, 3):
        other = (plane + step) % 4
        seven.append({"channel": other})
        seven.append({"tm": 1 - core, "channel": other})
    seven.append({"tm": 1 - core})

    def greet(peer):
        pl.semaphore_signal(barrier, inc=1, device_id=peer, device_id_type=MESH)

    everyone(lambda peer: greet({"station": peer}))
    for peer in seven:
        greet(peer)
    greet(three[0])
    for load in loads:
        load.start()
    row = lax.broadcasted_iota(jnp.int32, (8, 128), 0)
    upper = jnp.where(row < 4, 1.0, -1.0).astype(jnp.float32)

    for load in loads[:5]:
        load.wait()
    for c in range(8):
        left = []
        for p in range(2):
            real_s = seed[0, c, pl.ds(p, 4, stride=2), :].astype(jnp.float32)
            imag_s = seed[1, c, pl.ds(p, 4, stride=2), :].astype(jnp.float32)
            left.append(jnp.concatenate([real_s, imag_s], axis=0))
        left = jnp.concatenate(left, axis=1).astype(jnp.bfloat16)
        for side in range(2):
            right = local_x[c, side].reshape(64, 256)
            rows = jnp.dot(left, right, preferred_element_type=jnp.float32)
            share = half_swap(rows[:, 128:256]) + upper * rows[:, 0:128]
            first_out[2 * c + side] = share.astype(jnp.bfloat16)

    pl.semaphore_wait(barrier, GROUP - 1 + len(seven) + 1)

    def first_copy(peer):
        return pltpu.make_async_remote_copy(
            src_ref=first_out.at[peer],
            dst_ref=first_in.at[me],
            send_sem=send_first,
            recv_sem=recv_first,
            device_id={"station": peer},
            device_id_type=MESH,
        )

    def x_copy(peer):
        return pltpu.make_async_remote_copy(
            src_ref=local_x.at[peer // 2, peer % 2],
            dst_ref=field.at[me],
            send_sem=send_x,
            recv_sem=recv_x,
            device_id={"station": peer},
            device_id_type=MESH,
        )

    for peer in others[:3]:
        x_copy(peer).start()
    everyone(lambda peer: first_copy(peer).start())
    for peer in others[3:]:
        x_copy(peer).start()
    own_x = pltpu.make_async_copy(local_x.at[mine, half], field.at[me], local_sem.at[7])
    own_x.start()
    first_in[me] = first_out[me]

    loads[5].wait()
    loads[6].wait()
    number = plane * 8 + mine + 1
    norming = STATIONS**-0.5

    def weight_rows(block, carry):
        rows = pl.ds(pl.multiple_of(block * 32, 32), 32)
        index = (phases[rows, :] + delay[...]) * number
        wrapped = (index + PHASES // 2) & (PHASES - 1)
        u = (wrapped - PHASES // 2).astype(jnp.float32) * jnp.float32(2.0 / PHASES)
        v = u * u
        weights[0, rows, :] = horner(COS_TERMS, norming, v).astype(jnp.bfloat16)
        weights[1, rows, :] = (u * horner(SIN_TERMS, -norming, v)).astype(jnp.bfloat16)
        return carry

    lax.fori_loop(0, 16, weight_rows, 0)

    together(first_in, recv_first).wait()
    together(field, recv_x).wait()
    own_x.wait()

    def turned(c8):
        return jnp.concatenate([c8, half_swap(c8) * upper], axis=1)

    def apply_field(c8):
        left = jnp.concatenate(three_parts(turned(c8)), axis=0)
        right = field[...].reshape(1024, 256)
        rows = lax.dot_general(left, right, (((1,), (1,)), ((), ())), preferred_element_type=jnp.float32)
        return sum_of_three(rows)

    def coefficients(h8):
        left = jnp.concatenate(three_parts(h8), axis=0)
        rows = jnp.dot(left, field[...].reshape(1024, 256), preferred_element_type=jnp.float32)
        rows = sum_of_three(rows)
        return rows[:, 0:128] - upper * half_swap(rows[:, 128:256])

    def factor(h8):
        shifted = []
        for shift in range(4):
            moved = h8 * (pltpu.roll(h8, shift, 0) if shift else h8)
            lanes = moved[:, 0:128]
            for block in range(1, 8):
                lanes = lanes + moved[:, block * 128 : (block + 1) * 128]
            dots = jnp.broadcast_to(jnp.sum(lanes, axis=1, keepdims=True), (8, 128))
            swapped = half_swap(dots)
            shifted.append((dots + swapped, dots - swapped))

        def pick(rows, at):
            return jnp.broadcast_to(rows[at : at + 1, :], (8, 128))

        low = {}
        inverse = {}
        for column in range(RANK):
            diagonal = pick(shifted[0][0], column)
            for middle in range(column):
                re, im = low[column, middle]
                diagonal = diagonal - (re * re + im * im)
            inverse[column] = lax.rsqrt(diagonal)
            for at in range(column + 1, RANK):
                distance = at - column
                re = pick(shifted[distance][0], at)
                im = pick(shifted[4 - distance][1], column)
                for middle in range(column):
                    a_re, a_im = low[at, middle]
                    b_re, b_im = low[column, middle]
                    re = re - (a_re * b_re + a_im * b_im)
                    im = im - (a_im * b_re - a_re * b_im)
                low[at, column] = (re * inverse[column], im * inverse[column])
        return low, inverse

    def solve(low, inverse, rows):
        width = rows.shape[1]
        repeat = width // 128

        def wide(value):
            return value if repeat == 1 else jnp.concatenate([value] * repeat, axis=1)

        done = []
        for at in range(RANK):
            re = jnp.broadcast_to(rows[at : at + 1, :], (8, width))
            im = jnp.broadcast_to(rows[at + 4 : at + 5, :], (8, width))
            for middle in range(at):
                l_re, l_im = low[at, middle]
                l_re, l_im = wide(l_re), wide(l_im)
                d_re, d_im = done[middle]
                re = re - (l_re * d_re - l_im * d_im)
                im = im - (l_re * d_im + l_im * d_re)
            scale = wide(inverse[at])
            done.append((re * scale, im * scale))
        at_row = lax.broadcasted_iota(jnp.int32, (8, width), 0)
        total = done[3][1]
        for at in range(RANK):
            total = jnp.where(at_row == at, done[at][0], total)
            if at < 3:
                total = jnp.where(at_row == at + 4, done[at][1], total)
        return total

    coefficient = jnp.sum(first_in[...].astype(jnp.float32), axis=0)

    image_copies = []
    for iteration in range(ITERS):
        image[iteration, quarter] = apply_field(coefficient)
        for at, peer in enumerate(three):
            copy = pltpu.make_async_remote_copy(
                src_ref=image.at[iteration, quarter],
                dst_ref=image.at[iteration, quarter],
                send_sem=send_image.at[iteration, at],
                recv_sem=recv_image.at[iteration, at],
                device_id=peer,
                device_id_type=MESH,
            )
            copy.start()
            image_copies.append(copy)
        for copy in image_copies[-3:]:
            copy.wait_recv()
        summed = (image[iteration, 0] + image[iteration, 1]) + (image[iteration, 2] + image[iteration, 3])
        raw = coefficients(summed)
        low, inverse = factor(summed)
        coefficient = solve(low, inverse, raw)
    basis = solve(low, inverse, summed)

    def six(parts, which):
        return jnp.concatenate([parts[at] for at in which], axis=0)

    left = six(three_parts(basis), (0, 0, 1, 0, 1, 2))
    right = six(three_parts(turned(coefficient)), (0, 1, 0, 2, 1, 0))
    removed = lax.dot_general(left, right, (((0,), (0,)), ((), ())), preferred_element_type=jnp.float32)
    cleaned = field[...].reshape(1024, 256).astype(jnp.float32) - removed
    cleaned = cleaned.astype(jnp.bfloat16).reshape(GROUP, 2, 32, 256)
    lane_group = lax.broadcasted_iota(jnp.int32, (8, 128), 1) // 8
    compact = []
    kept_beams = []
    for block in range(8):
        lanes = basis[:, block * 128 : (block + 1) * 128] * upper
        compact += [pltpu.roll(lanes, 64, 1), lanes]
    for p in range(2):
        ours = cleaned[:, p].reshape(512, 256)
        on_real = jnp.dot(weights[0], ours, preferred_element_type=jnp.float32)
        on_imag = jnp.dot(weights[1], ours, preferred_element_type=jnp.float32)
        real_b = on_real[:, 0:128] - on_imag[:, 128:256]
        imag_b = on_real[:, 128:256] + on_imag[:, 0:128]
        kept_beams.append((real_b, imag_b))
        squares = jnp.sum(real_b * real_b + imag_b * imag_b, axis=1, keepdims=True)
        for station in range(GROUP):
            rows = slice(station * 32, (station + 1) * 32)
            for block in range(4):
                at = station * 32 + block * 8
                compact[station] = jnp.where(
                    lane_group == p * 4 + block,
                    jnp.broadcast_to(squares[at : at + 8], (8, 128)),
                    compact[station],
                )
    for station in range(GROUP):
        power_out[station] = compact[station]

    def power_copy(peer):
        return pltpu.make_async_remote_copy(
            src_ref=power_out.at[peer],
            dst_ref=power_in.at[me],
            send_sem=send_power,
            recv_sem=recv_power,
            device_id={"station": peer},
            device_id_type=MESH,
        )

    def beam_copy(peer):
        return pltpu.make_async_remote_copy(
            src_ref=stage.at[peer],
            dst_ref=arrived.at[me],
            send_sem=send_beam,
            recv_sem=recv_beam,
            device_id={"station": peer},
            device_id_type=MESH,
        )

    everyone(lambda peer: power_copy(peer).start())
    for p in range(2):
        for station in range(GROUP):
            rows = slice(station * 32, (station + 1) * 32)
            for part in range(2):
                stage[station, part, p] = kept_beams[p][part][rows].astype(jnp.bfloat16)
    for at in BEAM_TURNS:
        beam_copy(others[at]).start()
    power_in[me] = power_out[me]
    own_beam = pltpu.make_async_copy(stage.at[me], arrived.at[me], local_sem.at[8])
    own_beam.start()

    together(power_in, recv_power).wait()
    power = power_in[0]
    for station in range(1, GROUP):
        power = power + power_in[station]
    slot = plane * 2 + core
    power_two[slot] = power
    two_copies = []
    for at, peer in enumerate(seven):
        copy = pltpu.make_async_remote_copy(
            src_ref=power_two.at[slot],
            dst_ref=power_two.at[slot],
            send_sem=send_two.at[at],
            recv_sem=recv_two.at[at],
            device_id=peer,
            device_id_type=MESH,
        )
        copy.start()
        two_copies.append(copy)

    together(first_out, send_first).wait()
    together(field, send_x).wait()
    together(power_out, send_power).wait()
    for copy in image_copies:
        copy.wait_send()
    together(stage, send_beam).wait()
    together(arrived, recv_beam).wait()
    own_beam.wait()

    for copy in two_copies:
        copy.wait_recv()
    power = power_two[0]
    for at in range(1, 8):
        power = power + power_two[at]
    rescale[...] = lax.rsqrt(power / (CHANNELS * TIME) + 1e-06)

    for copy in two_copies:
        copy.wait_send()


def normalise(arrived, rescale, basis, out, sub_hbm, result, sub, sem):
    scales = []
    for p in range(2):
        rows = []
        for block in range(4):
            lane = (p * 4 + block) * 8
            rows.append(jnp.broadcast_to(rescale[:, lane : lane + 1], (8, 128)))
        scales.append(jnp.concatenate(rows, axis=0))
    copies = []
    for c in range(8):
        for side in range(2):
            for part in range(2):
                for p in range(2):
                    value = arrived[2 * c + side, part, p].astype(jnp.float32) * scales[p]
                    result[part, c, p, :, side * 128 : (side + 1) * 128] = value.astype(jnp.bfloat16)
        copy = pltpu.make_async_copy(result.at[:, c], out.at[:, c], sem.at[c])
        copy.start()
        copies.append(copy)
    for c in range(8):
        for p in range(2):
            for part in range(2):
                at = part * 4
                sub[part, c, pl.ds(p, 4, stride=2), :] = basis[2 * c, at : at + 4, 64 + p * 32 : 96 + p * 32]
    copy = pltpu.make_async_copy(sub, sub_hbm, sem.at[8])
    copy.start()
    copies.append(copy)
    for copy in copies:
        copy.wait()


def body(voltages, start_seed, beam_phase, station_delay):
    vmem = pl.BlockSpec(memory_space=pltpu.VMEM)
    hbm = pl.BlockSpec(memory_space=pltpu.MemorySpace.HBM)
    anywhere = pl.BlockSpec(memory_space=pl.ANY)
    dma = pltpu.SemaphoreType.DMA
    f32, bf16 = jnp.float32, jnp.bfloat16
    def kept(value):
        return pltpu.with_memory_space_constraint(value, pltpu.MemorySpace.HBM)

    operands = (
        voltages,
        start_seed.reshape(2, 8, 8, 32),
        beam_phase,
        station_delay.reshape(1, STATIONS),
    )
    arrived, rescale, basis = pl.pallas_call(
        exchange,
        out_shape=(
            jax.ShapeDtypeStruct((16, 2, 2, 32, 128), bf16),
            jax.ShapeDtypeStruct((8, 128), f32),
            jax.ShapeDtypeStruct((GROUP, 8, 128), f32),
        ),
        in_specs=[hbm] * 4,
        out_specs=(vmem, vmem, vmem),
        scratch_shapes=[
            pltpu.VMEM((8, 2, 2, 32, 256), bf16),
            pltpu.VMEM((2, 8, 8, 32), jnp.int32),
            pltpu.VMEM((512, 512), jnp.int32),
            pltpu.VMEM((1, 512), jnp.int32),
            pltpu.VMEM((GROUP, 2, 32, 256), bf16),
            pltpu.VMEM((GROUP, 8, 128), bf16),
            pltpu.VMEM((GROUP, 8, 128), bf16),
            pltpu.VMEM((ITERS, QUARTERS, 8, 1024), f32),
            pltpu.VMEM((2, 512, 512), bf16),
            pltpu.VMEM((GROUP, 2, 2, 32, 128), bf16),
            pltpu.VMEM((GROUP, 8, 128), f32),
            pltpu.VMEM((8, 8, 128), f32),
            dma((10,)),
            dma(()),
            dma(()),
            dma(()),
            dma(()),
            dma((ITERS, 3)),
            dma((ITERS, 3)),
            dma(()),
            dma(()),
            dma((7,)),
            dma((7,)),
            dma(()),
            dma(()),
        ],
        compiler_params=pltpu.CompilerParams(
            collective_id=0, has_side_effects=True, vmem_limit_bytes=40 * 1024 * 1024
        ),
    )(*map(kept, operands))
    beam_output, subspace = pl.pallas_call(
        normalise,
        out_shape=(
            jax.ShapeDtypeStruct((2, 8, 2, 32, 256), bf16),
            jax.ShapeDtypeStruct((2, 8, 8, 32), f32),
        ),
        in_specs=[vmem] * 3,
        out_specs=(anywhere, anywhere),
        scratch_shapes=[
            pltpu.VMEM((2, 8, 2, 32, 256), bf16),
            pltpu.VMEM((2, 8, 8, 32), f32),
            dma((9,)),
        ],
        compiler_params=pltpu.CompilerParams(vmem_limit_bytes=40 * 1024 * 1024),
    )(arrived, rescale, basis)
    return beam_output, subspace.reshape(2, 8, 4, 2, 32)


def solution(mesh):
    in_specs = (
        P(None, "channel", None, "station", "tm"),
        P(None, "channel", None, None, "station"),
        P(),
        P(),
    )
    out_specs = (
        P(None, "channel", None, "station", "tm"),
        P(None, "channel", None, None, "station"),
    )
    return jax.shard_map(body, mesh=mesh, in_specs=in_specs, out_specs=out_specs, check_vma=False)
```
